256 devices in a mesh: gx: 4 (over x), gy: 8 (over y, core), gz: 8 (over z).
Axes of the slice: x: 4, y: 4, z: 8, core: 2. Of those that a mesh axis runs over, the one named last changes fastest.
Arguments:
- residual_in: float32 [256, 512, 2048], P('gx', 'gy', 'gz'), may hold values from -700 to 700
Outputs:
- level_one: float32 [128, 256, 1024], P('gx', 'gy', 'gz')
- level_two: float32 [64, 128, 512], P('gx', 'gy', 'gz')
- level_three: float32 [32, 64, 256], P('gx', 'gy', 'gz')
- level_four: float32 [16, 32, 128], P('gx', 'gy', 'gz')
- level_five: float32 [8, 16, 64], P('gx', 'gy', 'gz')
- level_scales: float32 [5], replicated
The draws below stay inside these ranges and needn't reach their ends.
All inputs are finite; a program needn't handle non-finite values.
Results may differ from the reference program's by a relative error of at most 0.0002.
Values sent between devices are 32-bit elements; how exact they have to be, the bound alone decides.
No kernel may reach another device: no remote copies, remote signals or barrier semaphores. Data moves between devices by JAX's collectives and lax.ppermute only.
A program may use at most 64 MiB of HBM per device.

```python
import math
import jax
import jax.numpy as jnp
from jax import lax

LEVELS = 5
NX = 256
NY = 512
NZ = 2048


def draw_residual_in(key, part):
    key_list = jax.random.split(key, 5)
    ramp_x = jnp.exp(0.5 * math.log(3.0) * jnp.arange(NX, dtype=jnp.float32) / max(NX - 1, 1))
    ramp_y = jnp.exp(0.5 * math.log(3.0) * jnp.arange(NY, dtype=jnp.float32) / max(NY - 1, 1))
    ramp_z = jnp.exp(0.5 * math.log(3.0) * jnp.arange(NZ, dtype=jnp.float32) / max(NZ - 1, 1))
    rough_x = jnp.exp(0.5 * math.log(10.0) * jax.random.uniform(key_list[0], (NX,), jnp.float32))
    rough_y = jnp.exp(0.5 * math.log(10.0) * jax.random.uniform(key_list[1], (NY,), jnp.float32))
    rough_z = jnp.exp(0.5 * math.log(10.0) * jax.random.uniform(key_list[2], (NZ,), jnp.float32))
    amplitude = (ramp_x * rough_x)[:, None, None] * (ramp_y * rough_y)[None, :, None] * (ramp_z * rough_z)[None, None, :]
    values = amplitude * jax.random.truncated_normal(key_list[4], -4.0, 4.0, (NX, NY, NZ), jnp.float32)
    return values.astype(jnp.float32)


def setup_inputs(seed: int = 0) -> dict:
    arg_keys = jax.random.split(jax.random.key(seed), 2)
    residual_in = draw_residual_in(jax.random.fold_in(arg_keys[1], 71), 0)
    return {"residual_in": residual_in}


WEIGHTS = (0.25, 0.5, 0.25)
EPSILON = 1e-06

def restrict_cube(values):
    half_x = values.shape[0] // 2
    half_y = values.shape[1] // 2
    half_z = values.shape[2] // 2
    padded = jnp.pad(values, ((1, 0), (1, 0), (1, 0)))
    summed = jnp.zeros((half_x, half_y, half_z), jnp.float32)
    for off_x in range(3):
        for off_y in range(3):
            for off_z in range(3):
                picked = lax.slice(padded, (off_x, off_y, off_z), (off_x + 2 * half_x - 1, off_y + 2 * half_y - 1, off_z + 2 * half_z - 1), (2, 2, 2))
                summed = summed + WEIGHTS[off_x] * WEIGHTS[off_y] * WEIGHTS[off_z] * picked
    return summed

def reference(residual_in):
    current = residual_in
    grid_list = []
    scale_list = []
    for step_no in range(LEVELS):
        coarse = restrict_cube(current)
        mean_sq = jnp.sum(coarse * coarse) / coarse.size
        scale_now = jnp.sqrt(mean_sq + EPSILON)
        current = coarse / scale_now
        grid_list.append(current)
        scale_list.append(scale_now)
    return (grid_list[0], grid_list[1], grid_list[2], grid_list[3], grid_list[4], jnp.stack(scale_list))
```

```python
import jax
import jax.numpy as jnp
from jax import lax
from jax.experimental import pallas as pl
from jax.experimental.pallas import tpu as pltpu
from jax.sharding import Mesh
from jax.sharding import PartitionSpec as P

LEVELS = 5
GY = ("gy_0", "gy_1")
GX_GY_GZ = ("gx", "gy_0", "gy_1", "gz")
EPSILON = 1e-06

BX, BY, BZ = 64, 64, 256
LANES = 128
CHUNK = 8
COUNT = [BX >> level for level in range(1, LEVELS + 1)]
ROWS = [40, 24, 16, 8, 8]
PASS_ROWS = [88, 56, 40, 24, 24]
REST_AT = [0, 0, 408, 552, 592]
REST_ROWS = 616
FIRST_ROWS = (COUNT[0] + 1) * ROWS[0]
LANE_AT = [0, 0, 64, 96, 112]
LANE_COUNT = [128, 64, 32, 16, 8]
END_AT = 120
FACE_AT = [-1, 30, 45, 52, 55]


def face_lane(level, plane):
    return END_AT + level if plane == 0 else FACE_AT[level] + plane


def iota(shape, dim):
    return lax.broadcasted_iota(jnp.int32, shape, dim)


def tile_mask(level, shape):
    lane = iota(shape, len(shape) - 1)
    return (lane >= LANE_AT[level]) & (lane < LANE_AT[level] + LANE_COUNT[level])


def face_mask(level, shape):
    lane = iota(shape, len(shape) - 1)
    first = FACE_AT[level] + 1
    return (lane == END_AT + level) | ((lane >= first) & (lane < first + COUNT[level] - 1))


def stencil_table():
    lane = iota((1, BZ), 1)
    width = jnp.zeros((1, BZ), jnp.float32)
    centre = jnp.zeros((1, BZ), jnp.float32)
    scale = jnp.zeros((1, BZ), jnp.float32)
    for level in range(LEVELS):
        step = 2 << level
        base = LANE_AT[level] + (LANES if level else 0)
        inside = (lane >= base) & (lane < base + LANE_COUNT[level])
        past = lane == LANES + END_AT + level
        width = jnp.where(inside | past, float(step), width)
        scale = jnp.where(inside | past, 1.0 / 64 ** (level + 1), scale)
        centre = jnp.where(inside, ((lane - base) * step).astype(jnp.float32), centre)
        centre = jnp.where(past, float(BZ), centre)
    row = iota((BZ, BZ), 0).astype(jnp.float32)
    return (jnp.maximum(width - jnp.abs(row - centre), 0.0) * scale).astype(jnp.bfloat16)


def apply_table(values, table):
    high = values.astype(jnp.bfloat16)
    low = (values - high.astype(jnp.float32)).astype(jnp.bfloat16)
    top = jnp.dot(high, table, preferred_element_type=jnp.float32)
    return top + jnp.dot(low, table, preferred_element_type=jnp.float32)


def aligned(start):
    return start if isinstance(start, int) else pl.multiple_of(start, 8)


def y_pass(pass_ref, plane, level):
    base = aligned(plane * PASS_ROWS[level]) + 8
    full = (COUNT[level] // 8) * 8
    parts = []
    if full:
        middle = pass_ref[pl.ds(base, full, stride=2), :]
        after = pass_ref[pl.ds(base + 1, full, stride=2), :]
        before = pass_ref[pl.ds(base - 1, full, stride=2), :]
        parts.append(before + after + (middle + middle))
    rest = ROWS[level] - full
    before = pass_ref[pl.ds(base + 2 * full - 1, rest, stride=2), :]
    if level:
        middle = pass_ref[pl.ds(base + 2 * full, rest, stride=2), :]
        before += middle + middle
    if not full:
        before += pass_ref[pl.ds(base + 1, rest, stride=2), :]
    parts.append(before)
    return parts[0] if len(parts) == 1 else jnp.concatenate(parts, axis=0)


def local_kernel(grid_ref, first_ref, rest_ref, xface_ref, yface_ref, zface_ref, *scratch):
    block_ref, plane_ref, stack_ref, end_ref, sems = scratch[:5]
    pass_refs = [scratch[5 + 2 * level : 7 + 2 * level] for level in range(LEVELS)]

    def chunk_copy(index):
        return pltpu.make_async_copy(
            grid_ref.at[pl.ds(index * CHUNK, CHUNK)],
            block_ref.at[pl.ds(index * CHUNK + 1, CHUNK)],
            sems.at[index],
        )

    chunks = BX // CHUNK
    for index in range(chunks):
        chunk_copy(index).start()
    table = stencil_table()
    block_ref[0] = jnp.zeros((BY, BZ), jnp.float32)
    for level in range(LEVELS):
        body = BY if level == 0 else ROWS[level - 1]
        tail = PASS_ROWS[level] - 8 - body
        for half in range(2):
            ref = pass_refs[level][half]
            for plane in range(COUNT[level] + 1):
                base = plane * PASS_ROWS[level]
                ref[pl.ds(base, 8), :] = jnp.zeros((8, LANES), jnp.float32)
                if tail:
                    ref[pl.ds(base + 8 + body, tail), :] = jnp.zeros((tail, LANES), jnp.float32)

    def first_y(plane):
        for half in range(2):
            lanes = slice(half * LANES, (half + 1) * LANES)
            out = y_pass(pass_refs[0][half], plane, 0)
            plane_ref[pl.ds(aligned(plane * ROWS[0]), ROWS[0]), lanes] = out

    def first_level(index, carry):
        chunk_copy(index).wait()
        for part in range(CHUNK // 2):
            plane = index * (CHUNK // 2) + part
            for half in range(2):
                lanes = slice(half * LANES, (half + 1) * LANES)
                before = block_ref[2 * plane, :, lanes]
                middle = block_ref[2 * plane + 1, :, lanes]
                after = block_ref[2 * plane + 2, :, lanes]
                pass_refs[0][half][pl.ds(aligned(plane * PASS_ROWS[0]) + 8, BY), :] = (
                    before + after + (middle + middle)
                )
        for part in range(CHUNK // 2):
            first_y(index * (CHUNK // 2) + part)
        return carry

    lax.fori_loop(0, chunks, first_level, 0)
    for half in range(2):
        lanes = slice(half * LANES, (half + 1) * LANES)
        pass_refs[0][half][pl.ds(COUNT[0] * PASS_ROWS[0] + 8, BY), :] = block_ref[BX, :, lanes]
    first_y(COUNT[0])

    for level in range(1, LEVELS):
        source = plane_ref if level == 1 else stack_ref
        source_at = REST_AT[level - 1] if level > 1 else 0
        rows = ROWS[level - 1]
        for half in range(2):
            lanes = slice(half * LANES, (half + 1) * LANES)
            ref = pass_refs[level][half]
            for plane in range(COUNT[level] + 1):
                middle = source[pl.ds(source_at + 2 * plane * rows, rows), lanes]
                total = middle + middle
                if plane > 0:
                    total += source[pl.ds(source_at + (2 * plane - 1) * rows, rows), lanes]
                if plane < COUNT[level]:
                    total += source[pl.ds(source_at + (2 * plane + 1) * rows, rows), lanes]
                ref[pl.ds(plane * PASS_ROWS[level] + 8, rows), :] = total
            for plane in range(COUNT[level] + 1):
                at = REST_AT[level] + plane * ROWS[level]
                stack_ref[pl.ds(at, ROWS[level]), lanes] = y_pass(ref, plane, level)

    span = 8 * ROWS[0]

    def first_z(index, carry):
        at = aligned(index * span)
        both = apply_table(plane_ref[pl.ds(at, span), :], table)
        first_ref[pl.ds(at, span), :] = both[:, :LANES]
        end_ref[pl.ds(at, span), :] = both[:, LANES:]
        return carry

    lax.fori_loop(0, COUNT[0] // 8, first_z, 0)
    last = COUNT[0] * ROWS[0]
    both = apply_table(plane_ref[pl.ds(last, ROWS[0]), :], table)
    first_ref[pl.ds(last, ROWS[0]), :] = both[:, :LANES]
    end_ref[pl.ds(last, ROWS[0]), :] = both[:, LANES:]
    rest_ref[...] = apply_table(stack_ref[...], table[:, LANES:])

    def right_rows(level, plane):
        ref = end_ref if level == 0 else rest_ref
        at = (0 if level == 0 else REST_AT[level]) + plane * ROWS[level]
        return ref[pl.ds(at, ROWS[level]), :]

    xface_ref[:, :LANES] = first_ref[pl.ds(last, ROWS[0]), :]
    tile = jnp.where(iota((ROWS[0], LANES), 1) == END_AT, right_rows(0, COUNT[0]), 0.0)
    xface_ref[:, LANES:] = tile
    for level in range(1, LEVELS):
        shape = (ROWS[level], LANES)
        keep = tile_mask(level, shape) | (iota(shape, 1) == END_AT + level)
        old = xface_ref[pl.ds(0, ROWS[level]), LANES:]
        xface_ref[pl.ds(0, ROWS[level]), LANES:] = jnp.where(keep, right_rows(level, COUNT[level]), old)

    yface_ref[:, :LANES] = first_ref[pl.ds(COUNT[0], COUNT[0], stride=ROWS[0]), :]
    yface_ref[:, LANES:] = jnp.zeros((COUNT[0], LANES), jnp.float32)
    for level in range(1, LEVELS):
        count = COUNT[level]
        at = REST_AT[level] + count
        if count >= 8:
            new = rest_ref[pl.ds(at, count, stride=ROWS[level]), :]
        else:
            new = jnp.zeros((8, LANES), jnp.float32)
            for plane in range(count):
                row = rest_ref[pl.ds(at + plane * ROWS[level], 1), :]
                new = jnp.where(iota((8, LANES), 0) == plane, row, new)
        size = max(count, 8)
        old = yface_ref[pl.ds(0, size), LANES:]
        yface_ref[pl.ds(0, size), LANES:] = jnp.where(tile_mask(level, (size, LANES)), new, old)

    total = None
    for level in range(LEVELS):
        lane = iota((ROWS[level], LANES), 1)
        face = jnp.zeros((ROWS[level], LANES), jnp.float32)
        for plane in range(COUNT[level]):
            values = right_rows(level, plane)
            target = face_lane(level, plane)
            shift = (target - END_AT - level) % LANES
            if shift:
                values = pltpu.roll(values, shift, 1)
            face = jnp.where(lane == target, values, face)
        if total is None:
            zface_ref[...] = face
            total = True
        else:
            zface_ref[pl.ds(0, ROWS[level]), :] = zface_ref[pl.ds(0, ROWS[level]), :] + face


def local_restriction(block):
    f32 = jnp.float32
    scratch = [
        pltpu.VMEM((BX + 1, BY, BZ), f32),
        pltpu.VMEM((FIRST_ROWS, BZ), f32),
        pltpu.VMEM((REST_ROWS, BZ), f32),
        pltpu.VMEM((FIRST_ROWS, LANES), f32),
        pltpu.SemaphoreType.DMA((BX // CHUNK,)),
    ]
    for level in range(LEVELS):
        shape = ((COUNT[level] + 1) * PASS_ROWS[level], LANES)
        scratch += [pltpu.VMEM(shape, f32), pltpu.VMEM(shape, f32)]
    vmem = pl.BlockSpec(memory_space=pltpu.VMEM)
    return pl.pallas_call(
        local_kernel,
        out_shape=(
            jax.ShapeDtypeStruct((FIRST_ROWS, LANES), f32),
            jax.ShapeDtypeStruct((REST_ROWS, LANES), f32),
            jax.ShapeDtypeStruct((ROWS[0], BZ), f32),
            jax.ShapeDtypeStruct((COUNT[0], BZ), f32),
            jax.ShapeDtypeStruct((ROWS[0], LANES), f32),
        ),
        in_specs=[pl.BlockSpec(memory_space=pl.ANY)],
        out_specs=(vmem,) * 5,
        scratch_shapes=scratch,
        name="local_levels",
    )(block)


def edge_kernel(xin_ref, yface_ref, zface_ref, yout_ref, zout_ref):
    count = COUNT[0]
    lane = iota((ROWS[0], LANES), 1)
    zface = zface_ref[...] + jnp.where(lane >= END_AT, xin_ref[:, LANES:], 0.0)
    zout_ref[...] = zface
    row = iota((count, LANES), 0)
    yout_ref[pl.ds(0, count), :LANES] = yface_ref[:, :LANES] + jnp.where(
        row == 0, xin_ref[pl.ds(count, 1), :LANES], 0.0
    )
    edge = jnp.zeros((1, LANES), jnp.float32)
    corner = jnp.zeros((1, LANES), jnp.float32)
    for level in range(LEVELS):
        at = pl.ds(COUNT[level], 1)
        if level:
            edge = jnp.where(tile_mask(level, (1, LANES)), xin_ref[at, LANES:], edge)
        corner = jnp.where(face_mask(level, (1, LANES)), zout_ref[at, :], corner)
    yout_ref[pl.ds(0, count), LANES:] = yface_ref[:, LANES:] + jnp.where(row == 0, edge, 0.0)
    yout_ref[pl.ds(count, 8), :LANES] = jnp.where(iota((8, LANES), 0) == 0, corner, 0.0)
    yout_ref[pl.ds(count, 8), LANES:] = jnp.zeros((8, LANES), jnp.float32)


def add_edges(xin, yface, zface):
    f32 = jnp.float32
    vmem = pl.BlockSpec(memory_space=pltpu.VMEM)
    return pl.pallas_call(
        edge_kernel,
        out_shape=(
            jax.ShapeDtypeStruct((ROWS[0], BZ), f32),
            jax.ShapeDtypeStruct((ROWS[0], LANES), f32),
        ),
        in_specs=[vmem] * 3,
        out_specs=(vmem,) * 2,
        name="edges",
    )(xin, yface, zface)


def finish_kernel(first_ref, rest_ref, xin_ref, yin_ref, zin_ref, *out_refs):
    sums_ref = out_refs[LEVELS]
    sums = jnp.zeros((1, LANES), jnp.float32)
    for level in range(LEVELS):
        count = COUNT[level]
        rows = max(count, 8)
        half = slice(0, LANES) if level == 0 else slice(LANES, 2 * LANES)
        source = first_ref if level == 0 else rest_ref
        shape = (rows, LANES)
        inside = tile_mask(level, shape) & (iota(shape, 0) < count)
        zlane = iota(shape, 1) == LANE_AT[level]
        squares = jnp.zeros((8, LANES), jnp.float32)
        for plane in range(count):
            at = REST_AT[level] + plane * ROWS[level]
            values = source[pl.ds(at, rows), :]
            if plane == 0:
                values = values + xin_ref[pl.ds(0, rows), half]
            yrow = jnp.where(iota((8, LANES), 0) == 0, yin_ref[pl.ds(plane, 1), half], 0.0)
            if rows > 8:
                yrow = jnp.concatenate([yrow, jnp.zeros((rows - 8, LANES), jnp.float32)], axis=0)
            shift = (LANE_AT[level] - face_lane(level, plane)) % LANES
            zcol = zin_ref[pl.ds(0, rows), :]
            if shift:
                zcol = pltpu.roll(zcol, shift, 1)
            values = values + yrow + jnp.where(zlane, zcol, 0.0)
            if level:
                values = jnp.where(inside, values, 0.0)
            out_refs[level][plane] = values
            squared = values * values
            for tile in range(rows // 8):
                squares = squares + squared[tile * 8 : tile * 8 + 8]
        total = jnp.sum(jnp.sum(squares, axis=0, keepdims=True), axis=1, keepdims=True)
        sums = jnp.where(iota((1, LANES), 1) == level, total, sums)
    sums_ref[...] = jnp.broadcast_to(sums, sums_ref.shape)


def finish_levels(first, rest, xin, yin, zin, devices):
    f32 = jnp.float32
    vmem = pl.BlockSpec(memory_space=pltpu.VMEM)
    shapes = [(COUNT[level], max(COUNT[level], 8), LANES) for level in range(LEVELS)]
    shapes.append((devices, LANES))
    return pl.pallas_call(
        finish_kernel,
        out_shape=tuple(jax.ShapeDtypeStruct(shape, f32) for shape in shapes),
        in_specs=[vmem] * 5,
        out_specs=(vmem,) * 6,
        name="finish",
    )(first, rest, xin, yin, zin)


def scale_kernel(sums_ref, *refs):
    level_refs = refs[:LEVELS]
    out_refs = refs[LEVELS : 2 * LEVELS]
    scales_ref = refs[2 * LEVELS]
    devices = sums_ref.shape[0]
    totals = jnp.sum(sums_ref[...], axis=0, keepdims=True)
    lane = iota((1, LANES), 1)
    product = jnp.ones((1, 1), jnp.float32)
    scales = jnp.zeros((1, LANES), jnp.float32)
    for level in range(LEVELS):
        cells = COUNT[level] * COUNT[level] * LANE_COUNT[level] * devices
        total = jnp.sum(jnp.where(lane == level, totals, 0.0), axis=1, keepdims=True)
        scale = jnp.sqrt(total / (product * product) * (1.0 / cells) + EPSILON)
        product = product * scale
        scales = jnp.where(lane == level, scale, scales)
        factor = jnp.broadcast_to(1.0 / product, (8, LANES))
        count = COUNT[level]
        for plane in range(count):
            for tile in range(max(count // 8, 1)):
                values = level_refs[level][plane, pl.ds(tile * 8, 8), :] * factor
                if LANE_AT[level]:
                    values = pltpu.roll(values, LANES - LANE_AT[level], 1)
                size = min(count, 8)
                out_refs[level][plane, pl.ds(tile * 8, size), :] = values[:size, : LANE_COUNT[level]]
    scales_ref[...] = scales[0, :LEVELS]


def scale_levels(sums, levels):
    f32 = jnp.float32
    vmem = pl.BlockSpec(memory_space=pltpu.VMEM)
    shapes = [(COUNT[level], COUNT[level], LANE_COUNT[level]) for level in range(LEVELS)]
    shapes.append((LEVELS,))
    return pl.pallas_call(
        scale_kernel,
        out_shape=tuple(jax.ShapeDtypeStruct(shape, f32) for shape in shapes),
        in_specs=[vmem] * 6,
        out_specs=(vmem,) * 6,
        name="scale",
    )(sums, *levels)


def to_next(face, axis):
    return lax.ppermute(face, axis, [(i, i + 1) for i in range(lax.axis_size(axis) - 1)])


def per_device(residual_in):
    devices = lax.axis_size(GX_GY_GZ)
    first, rest, xface, yface, zface = local_restriction(residual_in)
    xin = to_next(xface, "gx")
    yface, zface = add_edges(xin, yface, zface)
    yin = to_next(yface, GY)
    corner = jnp.where(iota((COUNT[0], LANES), 0) == 0, yin[COUNT[0], :LANES], 0.0)
    zin = to_next(zface[: COUNT[0]] + corner, "gz")
    *levels, sums = finish_levels(first, rest, xin, yin, zin, devices)
    sums = lax.all_to_all(sums, GX_GY_GZ, 0, 0, tiled=True)
    return tuple(scale_levels(sums, levels))


def solution(mesh):
    torus = Mesh(
        mesh.devices.reshape(mesh.shape["gx"], mesh.shape["gy"] // 2, 2, mesh.shape["gz"]), GX_GY_GZ
    )
    placed = P("gx", GY, "gz")
    return jax.shard_map(
        per_device,
        mesh=torus,
        in_specs=(placed,),
        out_specs=(placed,) * LEVELS + (P(),),
        check_vma=False,
    )
```

```python
import math

import jax
import jax.numpy as jnp
from jax import lax
from jax.experimental import pallas as pl
from jax.experimental.pallas import tpu as pltpu
from jax.sharding import Mesh
from jax.sharding import PartitionSpec as P

LEVELS = 5
GX = ("gx",)
GY = ("gy_0", "gy_1")
GZ = ("gz",)
GX_GY_GZ = ("gx", "gy_0", "gy_1", "gz")
EPSILON = 1e-06

BX, BY, BZ = 64, 64, 256
LANES = 128
CHUNK = 8
COUNT = [BX >> level for level in range(1, LEVELS + 1)]
ROWS = [40, 24, 16, 8, 8]
PASS_ROWS = [88, 56, 40, 24, 24]
REST_AT = [0, 0, 408, 552, 592]
REST_ROWS = 616
FIRST_ROWS = (COUNT[0] + 1) * ROWS[0]
LANE_AT = [0, 0, 64, 96, 112]
LANE_COUNT = [128, 64, 32, 16, 8]
END_AT = 120
FACE_AT = [-1, 30, 45, 52, 55]


def face_lane(level, plane):
    return END_AT + level if plane == 0 else FACE_AT[level] + plane


def iota(shape, dim):
    return lax.broadcasted_iota(jnp.int32, shape, dim)


def tile_mask(level, shape):
    lane = iota(shape, len(shape) - 1)
    return (lane >= LANE_AT[level]) & (lane < LANE_AT[level] + LANE_COUNT[level])


def face_mask(level, shape):
    lane = iota(shape, len(shape) - 1)
    first = FACE_AT[level] + 1
    return (lane == END_AT + level) | ((lane >= first) & (lane < first + COUNT[level] - 1))


def stencil_table():
    lane = iota((1, BZ), 1)
    width = jnp.zeros((1, BZ), jnp.float32)
    centre = jnp.zeros((1, BZ), jnp.float32)
    scale = jnp.zeros((1, BZ), jnp.float32)
    for level in range(LEVELS):
        step = 2 << level
        base = LANE_AT[level] + (LANES if level else 0)
        inside = (lane >= base) & (lane < base + LANE_COUNT[level])
        past = lane == LANES + END_AT + level
        width = jnp.where(inside | past, float(step), width)
        scale = jnp.where(inside | past, 1.0 / 64 ** (level + 1), scale)
        centre = jnp.where(inside, ((lane - base) * step).astype(jnp.float32), centre)
        centre = jnp.where(past, float(BZ), centre)
    row = iota((BZ, BZ), 0).astype(jnp.float32)
    return (jnp.maximum(width - jnp.abs(row - centre), 0.0) * scale).astype(jnp.bfloat16)


def apply_table(values, table):
    high = values.astype(jnp.bfloat16)
    low = (values - high.astype(jnp.float32)).astype(jnp.bfloat16)
    top = jnp.dot(high, table, preferred_element_type=jnp.float32)
    return top + jnp.dot(low, table, preferred_element_type=jnp.float32)


def aligned(start):
    return start if isinstance(start, int) else pl.multiple_of(start, 8)


def y_pass(pass_ref, plane, level):
    base = aligned(plane * PASS_ROWS[level]) + 8
    full = (COUNT[level] // 8) * 8
    parts = []
    if full:
        middle = pass_ref[pl.ds(base, full, stride=2), :]
        after = pass_ref[pl.ds(base + 1, full, stride=2), :]
        before = pass_ref[pl.ds(base - 1, full, stride=2), :]
        parts.append(before + after + (middle + middle))
    rest = ROWS[level] - full
    before = pass_ref[pl.ds(base + 2 * full - 1, rest, stride=2), :]
    if level:
        middle = pass_ref[pl.ds(base + 2 * full, rest, stride=2), :]
        before += middle + middle
    if not full:
        before += pass_ref[pl.ds(base + 1, rest, stride=2), :]
    parts.append(before)
    return parts[0] if len(parts) == 1 else jnp.concatenate(parts, axis=0)


def local_kernel(grid_ref, first_ref, rest_ref, xface_ref, yface_ref, zface_ref, *scratch):
    block_ref, plane_ref, stack_ref, end_ref, sems = scratch[:5]
    pass_refs = [scratch[5 + 2 * level : 7 + 2 * level] for level in range(LEVELS)]

    def chunk_copy(index):
        return pltpu.make_async_copy(
            grid_ref.at[pl.ds(index * CHUNK, CHUNK)],
            block_ref.at[pl.ds(index * CHUNK + 1, CHUNK)],
            sems.at[index],
        )

    chunks = BX // CHUNK
    for index in range(chunks):
        chunk_copy(index).start()
    table = stencil_table()
    block_ref[0] = jnp.zeros((BY, BZ), jnp.float32)
    for level in range(LEVELS):
        body = BY if level == 0 else ROWS[level - 1]
        tail = PASS_ROWS[level] - 8 - body
        for half in range(2):
            ref = pass_refs[level][half]
            for plane in range(COUNT[level] + 1):
                base = plane * PASS_ROWS[level]
                ref[pl.ds(base, 8), :] = jnp.zeros((8, LANES), jnp.float32)
                if tail:
                    ref[pl.ds(base + 8 + body, tail), :] = jnp.zeros((tail, LANES), jnp.float32)

    def first_y(plane):
        for half in range(2):
            lanes = slice(half * LANES, (half + 1) * LANES)
            out = y_pass(pass_refs[0][half], plane, 0)
            plane_ref[pl.ds(aligned(plane * ROWS[0]), ROWS[0]), lanes] = out

    def first_level(index, carry):
        chunk_copy(index).wait()
        for part in range(CHUNK // 2):
            plane = index * (CHUNK // 2) + part
            for half in range(2):
                lanes = slice(half * LANES, (half + 1) * LANES)
                before = block_ref[2 * plane, :, lanes]
                middle = block_ref[2 * plane + 1, :, lanes]
                after = block_ref[2 * plane + 2, :, lanes]
                pass_refs[0][half][pl.ds(aligned(plane * PASS_ROWS[0]) + 8, BY), :] = (
                    before + after + (middle + middle)
                )
        for part in range(CHUNK // 2):
            first_y(index * (CHUNK // 2) + part)
        return carry

    lax.fori_loop(0, chunks, first_level, 0)
    for half in range(2):
        lanes = slice(half * LANES, (half + 1) * LANES)
        pass_refs[0][half][pl.ds(COUNT[0] * PASS_ROWS[0] + 8, BY), :] = block_ref[BX, :, lanes]
    first_y(COUNT[0])

    for level in range(1, LEVELS):
        source = plane_ref if level == 1 else stack_ref
        source_at = REST_AT[level - 1] if level > 1 else 0
        rows = ROWS[level - 1]
        for half in range(2):
            lanes = slice(half * LANES, (half + 1) * LANES)
            ref = pass_refs[level][half]
            for plane in range(COUNT[level] + 1):
                middle = source[pl.ds(source_at + 2 * plane * rows, rows), lanes]
                total = middle + middle
                if plane > 0:
                    total += source[pl.ds(source_at + (2 * plane - 1) * rows, rows), lanes]
                if plane < COUNT[level]:
                    total += source[pl.ds(source_at + (2 * plane + 1) * rows, rows), lanes]
                ref[pl.ds(plane * PASS_ROWS[level] + 8, rows), :] = total
            for plane in range(COUNT[level] + 1):
                at = REST_AT[level] + plane * ROWS[level]
                stack_ref[pl.ds(at, ROWS[level]), lanes] = y_pass(ref, plane, level)

    span = 8 * ROWS[0]

    def first_z(index, carry):
        at = aligned(index * span)
        both = apply_table(plane_ref[pl.ds(at, span), :], table)
        first_ref[pl.ds(at, span), :] = both[:, :LANES]
        end_ref[pl.ds(at, span), :] = both[:, LANES:]
        return carry

    lax.fori_loop(0, COUNT[0] // 8, first_z, 0)
    last = COUNT[0] * ROWS[0]
    both = apply_table(plane_ref[pl.ds(last, ROWS[0]), :], table)
    first_ref[pl.ds(last, ROWS[0]), :] = both[:, :LANES]
    end_ref[pl.ds(last, ROWS[0]), :] = both[:, LANES:]
    rest_ref[...] = apply_table(stack_ref[...], table[:, LANES:])

    def right_rows(level, plane):
        ref = end_ref if level == 0 else rest_ref
        at = (0 if level == 0 else REST_AT[level]) + plane * ROWS[level]
        return ref[pl.ds(at, ROWS[level]), :]

    keep_x = sends(GX)
    xface_ref[:, :LANES] = first_ref[pl.ds(last, ROWS[0]), :]
    tile = jnp.where(iota((ROWS[0], LANES), 1) == END_AT, right_rows(0, COUNT[0]), 0.0)
    xface_ref[:, LANES:] = tile
    for level in range(1, LEVELS):
        shape = (ROWS[level], LANES)
        keep = tile_mask(level, shape) | (iota(shape, 1) == END_AT + level)
        old = xface_ref[pl.ds(0, ROWS[level]), LANES:]
        xface_ref[pl.ds(0, ROWS[level]), LANES:] = jnp.where(keep, right_rows(level, COUNT[level]), old)
    xface_ref[...] = xface_ref[...] * keep_x

    yface_ref[:, :LANES] = first_ref[pl.ds(COUNT[0], COUNT[0], stride=ROWS[0]), :]
    yface_ref[:, LANES:] = jnp.zeros((COUNT[0], LANES), jnp.float32)
    for level in range(1, LEVELS):
        count = COUNT[level]
        at = REST_AT[level] + count
        if count >= 8:
            new = rest_ref[pl.ds(at, count, stride=ROWS[level]), :]
        else:
            new = jnp.zeros((8, LANES), jnp.float32)
            for plane in range(count):
                row = rest_ref[pl.ds(at + plane * ROWS[level], 1), :]
                new = jnp.where(iota((8, LANES), 0) == plane, row, new)
        size = max(count, 8)
        old = yface_ref[pl.ds(0, size), LANES:]
        yface_ref[pl.ds(0, size), LANES:] = jnp.where(tile_mask(level, (size, LANES)), new, old)

    total = None
    for level in range(LEVELS):
        lane = iota((ROWS[level], LANES), 1)
        face = jnp.zeros((ROWS[level], LANES), jnp.float32)
        for plane in range(COUNT[level]):
            values = right_rows(level, plane)
            target = face_lane(level, plane)
            shift = (target - END_AT - level) % LANES
            if shift:
                values = pltpu.roll(values, shift, 1)
            face = jnp.where(lane == target, values, face)
        if total is None:
            zface_ref[...] = face
            total = True
        else:
            zface_ref[pl.ds(0, ROWS[level]), :] = zface_ref[pl.ds(0, ROWS[level]), :] + face


def local_restriction(block):
    f32 = jnp.float32
    scratch = [
        pltpu.VMEM((BX + 1, BY, BZ), f32),
        pltpu.VMEM((FIRST_ROWS, BZ), f32),
        pltpu.VMEM((REST_ROWS, BZ), f32),
        pltpu.VMEM((FIRST_ROWS, LANES), f32),
        pltpu.SemaphoreType.DMA((BX // CHUNK,)),
    ]
    for level in range(LEVELS):
        shape = ((COUNT[level] + 1) * PASS_ROWS[level], LANES)
        scratch += [pltpu.VMEM(shape, f32), pltpu.VMEM(shape, f32)]
    vmem = pl.BlockSpec(memory_space=pltpu.VMEM)
    return pl.pallas_call(
        local_kernel,
        out_shape=(
            pltpu.VMEM((FIRST_ROWS, LANES), f32),
            pltpu.VMEM((REST_ROWS, LANES), f32),
            pltpu.VMEM((ROWS[0], BZ), f32),
            pltpu.VMEM((COUNT[0], BZ), f32),
            pltpu.VMEM((ROWS[0], LANES), f32),
        ),
        in_specs=[pl.BlockSpec(memory_space=pl.ANY)],
        out_specs=(vmem,) * 5,
        scratch_shapes=scratch,
        name="local_levels",
    )(block)


def edge_kernel(xin_ref, yface_ref, zface_ref, yout_ref, zout_ref, yzout_ref):
    count = COUNT[0]
    lane = iota((ROWS[0], LANES), 1)
    zface = zface_ref[...] + jnp.where(lane >= END_AT, xin_ref[:, LANES:], 0.0)
    keep_y = sends(GY)
    keep_z = sends(GZ)
    zout_ref[...] = zface[:count] * keep_z
    row = iota((count, LANES), 0)
    yout_ref[:, :LANES] = (
        yface_ref[:, :LANES] + jnp.where(row == 0, xin_ref[pl.ds(count, 1), :LANES], 0.0)
    ) * keep_y
    edge = jnp.zeros((1, LANES), jnp.float32)
    corner = jnp.zeros((1, LANES), jnp.float32)
    for level in range(LEVELS):
        at = COUNT[level]
        if level:
            edge = jnp.where(tile_mask(level, (1, LANES)), xin_ref[pl.ds(at, 1), LANES:], edge)
        corner = jnp.where(face_mask(level, (1, LANES)), zface[at : at + 1], corner)
    yout_ref[:, LANES:] = (yface_ref[:, LANES:] + jnp.where(row == 0, edge, 0.0)) * keep_y
    yzout_ref[...] = jnp.where(iota((8, LANES), 0) == 0, corner, 0.0) * (keep_y * keep_z)


def sends(axis):
    index = 0
    for name in axis:
        index = index * lax.axis_size(name) + lax.axis_index(name)
    return jnp.where(index < lax.axis_size(axis) - 1, 1.0, 0.0)


def resident(*arrays):
    return [pltpu.with_memory_space_constraint(array, pltpu.VMEM) for array in arrays]


def add_edges(xin, yface, zface):
    f32 = jnp.float32
    vmem = pl.BlockSpec(memory_space=pltpu.VMEM)
    return pl.pallas_call(
        edge_kernel,
        out_shape=(
            pltpu.VMEM((COUNT[0], BZ), f32),
            pltpu.VMEM((COUNT[0], LANES), f32),
            pltpu.VMEM((8, LANES), f32),
        ),
        in_specs=[vmem] * 3,
        out_specs=(vmem,) * 3,
        name="edges",
    )(*resident(xin, yface, zface))


def finish_kernel(first_ref, rest_ref, xin_ref, yin_ref, zin_ref, yzin_ref, *out_refs):
    sums_ref = out_refs[LEVELS]
    corner = yzin_ref[...]
    zface = jnp.concatenate([zin_ref[pl.ds(0, 8), :] + corner, zin_ref[pl.ds(8, COUNT[0] - 8), :]], axis=0)
    sums = jnp.zeros((1, LANES), jnp.float32)
    for level in range(LEVELS):
        count = COUNT[level]
        rows = max(count, 8)
        half = slice(0, LANES) if level == 0 else slice(LANES, 2 * LANES)
        source = first_ref if level == 0 else rest_ref
        shape = (rows, LANES)
        inside = tile_mask(level, shape) & (iota(shape, 0) < count)
        zlane = iota(shape, 1) == LANE_AT[level]
        squares = jnp.zeros((8, LANES), jnp.float32)
        for plane in range(count):
            at = REST_AT[level] + plane * ROWS[level]
            values = source[pl.ds(at, rows), :]
            if plane == 0:
                values = values + xin_ref[pl.ds(0, rows), half]
            yrow = jnp.where(iota((8, LANES), 0) == 0, yin_ref[pl.ds(plane, 1), half], 0.0)
            if rows > 8:
                yrow = jnp.concatenate([yrow, jnp.zeros((rows - 8, LANES), jnp.float32)], axis=0)
            shift = (LANE_AT[level] - face_lane(level, plane)) % LANES
            zcol = zface[:rows]
            if shift:
                zcol = pltpu.roll(zcol, shift, 1)
            values = values + yrow + jnp.where(zlane, zcol, 0.0)
            if level:
                values = jnp.where(inside, values, 0.0)
            out_refs[level][plane] = values
            squared = values * values
            for tile in range(rows // 8):
                squares = squares + squared[tile * 8 : tile * 8 + 8]
        total = jnp.sum(jnp.sum(squares, axis=0, keepdims=True), axis=1, keepdims=True)
        sums = jnp.where(iota((1, LANES), 1) == level, total, sums)
    sums_ref[...] = jnp.broadcast_to(sums, sums_ref.shape)


def finish_levels(first, rest, xin, yin, zin, yzin, devices):
    f32 = jnp.float32
    vmem = pl.BlockSpec(memory_space=pltpu.VMEM)
    shapes = [(COUNT[level], max(COUNT[level], 8), LANES) for level in range(LEVELS)]
    shapes.append((devices, LANES))
    return pl.pallas_call(
        finish_kernel,
        out_shape=tuple(pltpu.VMEM(shape, f32) for shape in shapes),
        in_specs=[vmem] * 6,
        out_specs=(vmem,) * 6,
        name="finish",
    )(*resident(first, rest, xin, yin, zin, yzin))


def scale_kernel(sums_ref, *refs):
    level_refs = refs[:LEVELS]
    out_refs = refs[LEVELS : 2 * LEVELS]
    scales_ref = refs[2 * LEVELS]
    devices = sums_ref.shape[0]
    totals = jnp.sum(sums_ref[...], axis=0, keepdims=True)
    lane = iota((1, LANES), 1)
    product = jnp.ones((1, 1), jnp.float32)
    scales = jnp.zeros((1, LANES), jnp.float32)
    for level in range(LEVELS):
        cells = COUNT[level] * COUNT[level] * LANE_COUNT[level] * devices
        total = jnp.sum(jnp.where(lane == level, totals, 0.0), axis=1, keepdims=True)
        scale = jnp.sqrt(total / (product * product) * (1.0 / cells) + EPSILON)
        product = product * scale
        scales = jnp.where(lane == level, scale, scales)
        factor = jnp.broadcast_to(1.0 / product, (8, LANES))
        count = COUNT[level]
        for plane in range(count):
            for tile in range(max(count // 8, 1)):
                values = level_refs[level][plane, pl.ds(tile * 8, 8), :] * factor
                if LANE_AT[level]:
                    values = pltpu.roll(values, LANES - LANE_AT[level], 1)
                size = min(count, 8)
                out_refs[level][plane, pl.ds(tile * 8, size), :] = values[:size, : LANE_COUNT[level]]
    scales_ref[...] = scales[0, :LEVELS]


def scale_levels(sums, levels):
    f32 = jnp.float32
    vmem = pl.BlockSpec(memory_space=pltpu.VMEM)
    shapes = [(COUNT[level], COUNT[level], LANE_COUNT[level]) for level in range(LEVELS)]
    shapes.append((LEVELS,))
    return pl.pallas_call(
        scale_kernel,
        out_shape=tuple(jax.ShapeDtypeStruct(shape, f32) for shape in shapes),
        in_specs=[vmem] * 6,
        out_specs=(vmem,) * 6,
        name="scale",
    )(*resident(sums, *levels))


def to_next(face, *axes):
    sizes = [lax.axis_size(axis) for axis in axes]
    route = []
    for source in range(math.prod(sizes)):
        target, rest, scale = 0, source, 1
        for size in reversed(sizes):
            target += (rest % size + 1) % size * scale
            rest //= size
            scale *= size
        route.append((source, target))
    return lax.ppermute(face, sum(axes, ()), route)


def per_device(residual_in):
    devices = lax.axis_size(GX_GY_GZ)
    first, rest, xface, yface, zface = local_restriction(residual_in)
    xin = to_next(xface, GX)
    yface, zface, edge = add_edges(xin, yface, zface)
    yin, zin, edgein = to_next(yface, GY), to_next(zface, GZ), to_next(edge, GY, GZ)
    *levels, sums = finish_levels(first, rest, xin, yin, zin, edgein, devices)
    sums = lax.all_to_all(sums, GX_GY_GZ, 0, 0, tiled=True)
    return tuple(scale_levels(sums, levels))


def solution(mesh):
    torus = Mesh(
        mesh.devices.reshape(mesh.shape["gx"], mesh.shape["gy"] // 2, 2, mesh.shape["gz"]), GX_GY_GZ
    )
    placed = P("gx", GY, "gz")
    return jax.shard_map(
        per_device,
        mesh=torus,
        in_specs=(placed,),
        out_specs=(placed,) * LEVELS + (P(),),
        check_vma=False,
    )
```

```python
import math

import jax
import jax.numpy as jnp
from jax import lax
from jax.experimental import pallas as pl
from jax.experimental.pallas import tpu as pltpu
from jax.sharding import Mesh
from jax.sharding import PartitionSpec as P

LEVELS = 5
GX = ("gx",)
GY = ("gy_0", "gy_1")
GZ = ("gz",)
GX_GY_GZ = ("gx", "gy_0", "gy_1", "gz")
EPSILON = 1e-06

BX, BY, BZ = 64, 64, 256
LANES = 128
CHUNK = 8
COUNT = [BX >> level for level in range(1, LEVELS + 1)]
ROWS = [40, 24, 16, 8, 8]
PASS_ROWS = [88, 56, 40, 24, 24]
REST_AT = [0, 0, 408, 552, 592]
REST_ROWS = 616
FIRST_ROWS = (COUNT[0] + 1) * ROWS[0]
HIGH_PLANES = [17, 8, 4, 2, 1]
LOW_PLANES = [17, 9, 5, 3, 2]
LANE_AT = [0, 0, 64, 96, 112]
LANE_COUNT = [128, 64, 32, 16, 8]
END_AT = 120
FACE_AT = [-1, 30, 45, 52, 55]


def face_lane(level, plane):
    return END_AT + level if plane == 0 else FACE_AT[level] + plane


def iota(shape, dim):
    return lax.broadcasted_iota(jnp.int32, shape, dim)


def tile_mask(level, shape):
    lane = iota(shape, len(shape) - 1)
    return (lane >= LANE_AT[level]) & (lane < LANE_AT[level] + LANE_COUNT[level])


def face_mask(level, shape):
    lane = iota(shape, len(shape) - 1)
    first = FACE_AT[level] + 1
    return (lane == END_AT + level) | ((lane >= first) & (lane < first + COUNT[level] - 1))


def stencil_table():
    lane = iota((1, BZ), 1)
    width = jnp.zeros((1, BZ), jnp.float32)
    centre = jnp.zeros((1, BZ), jnp.float32)
    scale = jnp.zeros((1, BZ), jnp.float32)
    for level in range(LEVELS):
        step = 2 << level
        base = LANE_AT[level] + (LANES if level else 0)
        inside = (lane >= base) & (lane < base + LANE_COUNT[level])
        past = lane == LANES + END_AT + level
        width = jnp.where(inside | past, float(step), width)
        scale = jnp.where(inside | past, 1.0 / 64 ** (level + 1), scale)
        centre = jnp.where(inside, ((lane - base) * step).astype(jnp.float32), centre)
        centre = jnp.where(past, float(BZ), centre)
    row = iota((BZ, BZ), 0).astype(jnp.float32)
    return (jnp.maximum(width - jnp.abs(row - centre), 0.0) * scale).astype(jnp.bfloat16)


def apply_table(values, table):
    high = values.astype(jnp.bfloat16)
    low = (values - high.astype(jnp.float32)).astype(jnp.bfloat16)
    top = jnp.dot(high, table, preferred_element_type=jnp.float32)
    return top + jnp.dot(low, table, preferred_element_type=jnp.float32)


def aligned(start):
    return start if isinstance(start, int) else pl.multiple_of(start, 8)


def y_pass(pass_ref, plane, level):
    base = aligned(plane * PASS_ROWS[level]) + 8
    full = (COUNT[level] // 8) * 8
    parts = []
    if full:
        middle = pass_ref[pl.ds(base, full, stride=2), :]
        after = pass_ref[pl.ds(base + 1, full, stride=2), :]
        before = pass_ref[pl.ds(base - 1, full, stride=2), :]
        parts.append(before + after + (middle + middle))
    rest = ROWS[level] - full
    before = pass_ref[pl.ds(base + 2 * full - 1, rest, stride=2), :]
    if level:
        middle = pass_ref[pl.ds(base + 2 * full, rest, stride=2), :]
        before += middle + middle
    if not full:
        before += pass_ref[pl.ds(base + 1, rest, stride=2), :]
    parts.append(before)
    return parts[0] if len(parts) == 1 else jnp.concatenate(parts, axis=0)


def high_from(level):
    return COUNT[level] // 2 + 1


def pass_scratch(planes):
    shapes = [(count * PASS_ROWS[level], LANES) for level, count in enumerate(planes)]
    return [pltpu.VMEM(shape, jnp.float32) for shape in shapes for _ in range(2)]


def clear_rims(pass_refs, planes):
    for level in range(LEVELS):
        body = BY if level == 0 else ROWS[level - 1]
        tail = PASS_ROWS[level] - 8 - body
        for ref in pass_refs[2 * level : 2 * level + 2]:
            for plane in range(planes[level]):
                base = plane * PASS_ROWS[level]
                ref[pl.ds(base, 8), :] = jnp.zeros((8, LANES), jnp.float32)
                if tail:
                    ref[pl.ds(base + 8 + body, tail), :] = jnp.zeros((tail, LANES), jnp.float32)


def first_planes(block_ref, pass_refs, plane_ref, planes, offset):
    for plane in planes:
        for half in range(2):
            lanes = slice(half * LANES, (half + 1) * LANES)
            before = block_ref[2 * plane, :, lanes]
            middle = block_ref[2 * plane + 1, :, lanes]
            after = block_ref[2 * plane + 2, :, lanes]
            pass_refs[half][pl.ds(aligned(plane * PASS_ROWS[0]) + 8, BY), :] = (
                before + after + (middle + middle)
            )
    for plane in planes:
        first_y(pass_refs, plane_ref, plane, offset)


def first_y(pass_refs, plane_ref, plane, offset):
    for half in range(2):
        lanes = slice(half * LANES, (half + 1) * LANES)
        at = aligned((plane + offset) * ROWS[0])
        plane_ref[pl.ds(at, ROWS[0]), lanes] = y_pass(pass_refs[half], plane, 0)


def later_planes(level, planes, load, pass_refs, stack_ref):
    for half in range(2):
        lanes = slice(half * LANES, (half + 1) * LANES)
        ref = pass_refs[2 * level + half]
        for local, plane in enumerate(planes):
            middle = load(2 * plane, lanes)
            total = middle + middle
            if plane > 0:
                total += load(2 * plane - 1, lanes)
            if plane < COUNT[level]:
                total += load(2 * plane + 1, lanes)
            ref[pl.ds(local * PASS_ROWS[level] + 8, ROWS[level - 1]), :] = total
        for local, plane in enumerate(planes):
            at = REST_AT[level] + plane * ROWS[level]
            stack_ref[pl.ds(at, ROWS[level]), lanes] = y_pass(ref, local, level)


def high_kernel(grid_ref, plane_ref, stack_ref, xface_ref, block_ref, sems, *pass_refs):
    half_x = BX // 2
    chunks = half_x // CHUNK

    def chunk_copy(index):
        return pltpu.make_async_copy(
            grid_ref.at[pl.ds(half_x + index * CHUNK, CHUNK)],
            block_ref.at[pl.ds(index * CHUNK + 1, CHUNK)],
            sems.at[index],
        )

    for index in range(chunks):
        chunk_copy(index).start()
    table = stencil_table()
    block_ref[0] = jnp.zeros((BY, BZ), jnp.float32)
    clear_rims(pass_refs, HIGH_PLANES)

    def step(index, carry):
        chunk_copy(index).wait()
        planes = [index * (CHUNK // 2) + part for part in range(CHUNK // 2)]
        first_planes(block_ref, pass_refs, plane_ref, planes, COUNT[0] // 2)
        return carry

    lax.fori_loop(0, chunks, step, 0)
    for half in range(2):
        lanes = slice(half * LANES, (half + 1) * LANES)
        at = COUNT[0] // 2 * PASS_ROWS[0] + 8
        pass_refs[half][pl.ds(at, BY), :] = block_ref[half_x, :, lanes]
    first_y(pass_refs, plane_ref, COUNT[0] // 2, COUNT[0] // 2)
    for level in range(1, LEVELS):

        def load(plane, lanes, level=level):
            source = plane_ref if level == 1 else stack_ref
            at = (REST_AT[level - 1] if level > 1 else 0) + plane * ROWS[level - 1]
            return source[pl.ds(at, ROWS[level - 1]), lanes]

        later_planes(level, range(high_from(level), COUNT[level] + 1), load, pass_refs, stack_ref)

    keep_x = sends(GX)
    parts = [plane_ref[pl.ds(COUNT[0] * ROWS[0], ROWS[0]), :]]
    for level in range(1, LEVELS):
        parts.append(stack_ref[pl.ds(REST_AT[level] + COUNT[level] * ROWS[level], ROWS[level]), :])
    faces = apply_table(jnp.concatenate(parts, axis=0), table) * keep_x
    xface_ref[:, :LANES] = faces[: ROWS[0], :LANES]
    tiles = [jnp.where(iota((ROWS[0], LANES), 1) == END_AT, faces[: ROWS[0], LANES:], 0.0)]
    at = ROWS[0]
    for level in range(1, LEVELS):
        shape = (ROWS[level], LANES)
        keep = tile_mask(level, shape) | (iota(shape, 1) == END_AT + level)
        face = jnp.where(keep, faces[at : at + ROWS[level], LANES:], 0.0)
        at += ROWS[level]
        if ROWS[level] < ROWS[0]:
            blank = jnp.zeros((ROWS[0] - ROWS[level], LANES), jnp.float32)
            face = jnp.concatenate([face, blank], axis=0)
        tiles.append(face)
    xface_ref[:, LANES:] = sum(tiles[1:], tiles[0])


def high_half(block):
    f32 = jnp.float32
    vmem = pl.BlockSpec(memory_space=pltpu.VMEM)
    return pl.pallas_call(
        high_kernel,
        out_shape=(
            pltpu.VMEM((FIRST_ROWS, BZ), f32),
            pltpu.VMEM((REST_ROWS, BZ), f32),
            pltpu.VMEM((ROWS[0], BZ), f32),
        ),
        in_specs=[pl.BlockSpec(memory_space=pl.ANY)],
        out_specs=(vmem,) * 3,
        scratch_shapes=[
            pltpu.VMEM((BX // 2 + 1, BY, BZ), f32),
            pltpu.SemaphoreType.DMA((BX // 2 // CHUNK,)),
        ]
        + pass_scratch(HIGH_PLANES),
        name="high_half",
    )(block)


def low_kernel(grid_ref, high_ref, highs_ref, first_ref, rest_ref, yface_ref, zface_ref, *scratch):
    block_ref, plane_ref, stack_ref, end_ref, sems = scratch[:5]
    pass_refs = scratch[5:]
    half_x = BX // 2
    chunks = half_x // CHUNK
    low = high_from(0)

    def copy(start, size, index):
        return pltpu.make_async_copy(
            grid_ref.at[pl.ds(start, size)], block_ref.at[pl.ds(start + 1, size)], sems.at[index]
        )

    for index in range(chunks):
        copy(index * CHUNK, CHUNK, index).start()
    copy(half_x, 2, chunks).start()
    table = stencil_table()
    block_ref[0] = jnp.zeros((BY, BZ), jnp.float32)
    clear_rims(pass_refs, LOW_PLANES)
    for level in range(1, LEVELS):
        at = REST_AT[level] + high_from(level) * ROWS[level]
        size = (COUNT[level] + 1 - high_from(level)) * ROWS[level]
        stack_ref[pl.ds(at, size), :] = highs_ref[pl.ds(at, size), :]

    def first_z(source, at, size):
        both = apply_table(source[pl.ds(at, size), :], table)
        first_ref[pl.ds(at, size), :] = both[:, :LANES]
        end_ref[pl.ds(at, size), :] = both[:, LANES:]

    def high_z(index, carry):
        span = 5 * ROWS[0]
        first_z(high_ref, aligned(low * ROWS[0] + index * span), span)
        return carry

    lax.fori_loop(0, (COUNT[0] - low) // 5, high_z, 0)

    def step(index, carry):
        copy(index * CHUNK, CHUNK, index).wait()
        planes = [index * (CHUNK // 2) + part for part in range(CHUNK // 2)]
        first_planes(block_ref, pass_refs, plane_ref, planes, 0)
        span = CHUNK // 2 * ROWS[0]
        first_z(plane_ref, aligned(index * span), span)
        return carry

    lax.fori_loop(0, chunks, step, 0)
    copy(half_x, 2, chunks).wait()
    first_planes(block_ref, pass_refs, plane_ref, [low - 1], 0)
    first_z(plane_ref, (low - 1) * ROWS[0], ROWS[0])
    for level in range(1, LEVELS):

        def load(plane, lanes, level=level):
            if level == 1:
                source = plane_ref if plane < low else high_ref
                return source[pl.ds(plane * ROWS[0], ROWS[0]), lanes]
            return stack_ref[pl.ds(REST_AT[level - 1] + plane * ROWS[level - 1], ROWS[level - 1]), lanes]

        later_planes(level, range(high_from(level)), load, pass_refs, stack_ref)
    rest_ref[...] = apply_table(stack_ref[...], table[:, LANES:])

    def right_rows(level, plane):
        ref = end_ref if level == 0 else rest_ref
        at = (0 if level == 0 else REST_AT[level]) + plane * ROWS[level]
        return ref[pl.ds(at, ROWS[level]), :]

    yface_ref[:, :LANES] = first_ref[pl.ds(COUNT[0], COUNT[0], stride=ROWS[0]), :]
    yface_ref[:, LANES:] = jnp.zeros((COUNT[0], LANES), jnp.float32)
    for level in range(1, LEVELS):
        count = COUNT[level]
        at = REST_AT[level] + count
        if count >= 8:
            new = rest_ref[pl.ds(at, count, stride=ROWS[level]), :]
        else:
            new = jnp.zeros((8, LANES), jnp.float32)
            for plane in range(count):
                row = rest_ref[pl.ds(at + plane * ROWS[level], 1), :]
                new = jnp.where(iota((8, LANES), 0) == plane, row, new)
        size = max(count, 8)
        old = yface_ref[pl.ds(0, size), LANES:]
        yface_ref[pl.ds(0, size), LANES:] = jnp.where(tile_mask(level, (size, LANES)), new, old)

    for level in range(LEVELS):
        lane = iota((ROWS[level], LANES), 1)
        face = jnp.zeros((ROWS[level], LANES), jnp.float32)
        for plane in range(COUNT[level]):
            values = right_rows(level, plane)
            target = face_lane(level, plane)
            shift = (target - END_AT - level) % LANES
            if shift:
                values = pltpu.roll(values, shift, 1)
            face = jnp.where(lane == target, values, face)
        if level == 0:
            zface_ref[...] = face
        else:
            zface_ref[pl.ds(0, ROWS[level]), :] = zface_ref[pl.ds(0, ROWS[level]), :] + face


def low_half(block, high, highs):
    f32 = jnp.float32
    rows = COUNT[0] * ROWS[0]
    vmem = pl.BlockSpec(memory_space=pltpu.VMEM)
    return pl.pallas_call(
        low_kernel,
        out_shape=(
            pltpu.VMEM((rows, LANES), f32),
            pltpu.VMEM((REST_ROWS, LANES), f32),
            pltpu.VMEM((COUNT[0], BZ), f32),
            pltpu.VMEM((ROWS[0], LANES), f32),
        ),
        in_specs=[pl.BlockSpec(memory_space=pl.ANY), vmem, vmem],
        out_specs=(vmem,) * 4,
        scratch_shapes=[
            pltpu.VMEM((BX // 2 + 3, BY, BZ), f32),
            pltpu.VMEM((high_from(0) * ROWS[0], BZ), f32),
            pltpu.VMEM((REST_ROWS, BZ), f32),
            pltpu.VMEM((rows, LANES), f32),
            pltpu.SemaphoreType.DMA((BX // 2 // CHUNK + 1,)),
        ]
        + pass_scratch(LOW_PLANES),
        name="low_half",
    )(block, *resident(high, highs))


def edge_kernel(xin_ref, yface_ref, zface_ref, yout_ref, zout_ref, yzout_ref):
    count = COUNT[0]
    lane = iota((ROWS[0], LANES), 1)
    zface = zface_ref[...] + jnp.where(lane >= END_AT, xin_ref[:, LANES:], 0.0)
    keep_y = sends(GY)
    keep_z = sends(GZ)
    zout_ref[...] = zface[:count] * keep_z
    row = iota((count, LANES), 0)
    yout_ref[:, :LANES] = (
        yface_ref[:, :LANES] + jnp.where(row == 0, xin_ref[pl.ds(count, 1), :LANES], 0.0)
    ) * keep_y
    edge = jnp.zeros((1, LANES), jnp.float32)
    corner = jnp.zeros((1, LANES), jnp.float32)
    for level in range(LEVELS):
        at = COUNT[level]
        if level:
            edge = jnp.where(tile_mask(level, (1, LANES)), xin_ref[pl.ds(at, 1), LANES:], edge)
        corner = jnp.where(face_mask(level, (1, LANES)), zface[at : at + 1], corner)
    yout_ref[:, LANES:] = (yface_ref[:, LANES:] + jnp.where(row == 0, edge, 0.0)) * keep_y
    yzout_ref[...] = jnp.where(iota((8, LANES), 0) == 0, corner, 0.0) * (keep_y * keep_z)


def sends(axis):
    index = 0
    for name in axis:
        index = index * lax.axis_size(name) + lax.axis_index(name)
    return jnp.where(index < lax.axis_size(axis) - 1, 1.0, 0.0)


def resident(*arrays):
    return [pltpu.with_memory_space_constraint(array, pltpu.VMEM) for array in arrays]


def add_edges(xin, yface, zface):
    f32 = jnp.float32
    vmem = pl.BlockSpec(memory_space=pltpu.VMEM)
    return pl.pallas_call(
        edge_kernel,
        out_shape=(
            pltpu.VMEM((COUNT[0], BZ), f32),
            pltpu.VMEM((COUNT[0], LANES), f32),
            pltpu.VMEM((8, LANES), f32),
        ),
        in_specs=[vmem] * 3,
        out_specs=(vmem,) * 3,
        name="edges",
    )(*resident(xin, yface, zface))


def finish_kernel(first_ref, rest_ref, xin_ref, yin_ref, zin_ref, yzin_ref, *out_refs):
    sums_ref = out_refs[LEVELS]
    corner = yzin_ref[...]
    zface = jnp.concatenate([zin_ref[pl.ds(0, 8), :] + corner, zin_ref[pl.ds(8, COUNT[0] - 8), :]], axis=0)
    sums = jnp.zeros((1, LANES), jnp.float32)
    for level in range(LEVELS):
        count = COUNT[level]
        rows = max(count, 8)
        half = slice(0, LANES) if level == 0 else slice(LANES, 2 * LANES)
        source = first_ref if level == 0 else rest_ref
        shape = (rows, LANES)
        inside = tile_mask(level, shape) & (iota(shape, 0) < count)
        zlane = iota(shape, 1) == LANE_AT[level]
        squares = jnp.zeros((8, LANES), jnp.float32)
        for plane in range(count):
            at = REST_AT[level] + plane * ROWS[level]
            values = source[pl.ds(at, rows), :]
            if plane == 0:
                values = values + xin_ref[pl.ds(0, rows), half]
            yrow = jnp.where(iota((8, LANES), 0) == 0, yin_ref[pl.ds(plane, 1), half], 0.0)
            if rows > 8:
                yrow = jnp.concatenate([yrow, jnp.zeros((rows - 8, LANES), jnp.float32)], axis=0)
            shift = (LANE_AT[level] - face_lane(level, plane)) % LANES
            zcol = zface[:rows]
            if shift:
                zcol = pltpu.roll(zcol, shift, 1)
            values = values + yrow + jnp.where(zlane, zcol, 0.0)
            if level:
                values = jnp.where(inside, values, 0.0)
            out_refs[level][plane] = values
            squared = values * values
            for tile in range(rows // 8):
                squares = squares + squared[tile * 8 : tile * 8 + 8]
        total = jnp.sum(jnp.sum(squares, axis=0, keepdims=True), axis=1, keepdims=True)
        sums = jnp.where(iota((1, LANES), 1) == level, total, sums)
    sums_ref[...] = jnp.broadcast_to(sums, sums_ref.shape)


def finish_levels(first, rest, xin, yin, zin, yzin, devices):
    f32 = jnp.float32
    vmem = pl.BlockSpec(memory_space=pltpu.VMEM)
    shapes = [(COUNT[level], max(COUNT[level], 8), LANES) for level in range(LEVELS)]
    shapes.append((devices, LANES))
    return pl.pallas_call(
        finish_kernel,
        out_shape=tuple(pltpu.VMEM(shape, f32) for shape in shapes),
        in_specs=[vmem] * 6,
        out_specs=(vmem,) * 6,
        name="finish",
    )(*resident(first, rest, xin, yin, zin, yzin))


def scale_kernel(sums_ref, *refs):
    level_refs = refs[:LEVELS]
    out_refs = refs[LEVELS : 2 * LEVELS]
    scales_ref = refs[2 * LEVELS]
    devices = sums_ref.shape[0]
    totals = jnp.sum(sums_ref[...], axis=0, keepdims=True)
    lane = iota((1, LANES), 1)
    product = jnp.ones((1, 1), jnp.float32)
    scales = jnp.zeros((1, LANES), jnp.float32)
    for level in range(LEVELS):
        cells = COUNT[level] * COUNT[level] * LANE_COUNT[level] * devices
        total = jnp.sum(jnp.where(lane == level, totals, 0.0), axis=1, keepdims=True)
        scale = jnp.sqrt(total / (product * product) * (1.0 / cells) + EPSILON)
        product = product * scale
        scales = jnp.where(lane == level, scale, scales)
        factor = jnp.broadcast_to(1.0 / product, (8, LANES))
        count = COUNT[level]
        for plane in range(count):
            for tile in range(max(count // 8, 1)):
                values = level_refs[level][plane, pl.ds(tile * 8, 8), :] * factor
                if LANE_AT[level]:
                    values = pltpu.roll(values, LANES - LANE_AT[level], 1)
                size = min(count, 8)
                out_refs[level][plane, pl.ds(tile * 8, size), :] = values[:size, : LANE_COUNT[level]]
    scales_ref[...] = scales[0, :LEVELS]


def scale_levels(sums, levels):
    f32 = jnp.float32
    vmem = pl.BlockSpec(memory_space=pltpu.VMEM)
    shapes = [(COUNT[level], COUNT[level], LANE_COUNT[level]) for level in range(LEVELS)]
    shapes.append((LEVELS,))
    return pl.pallas_call(
        scale_kernel,
        out_shape=tuple(jax.ShapeDtypeStruct(shape, f32) for shape in shapes),
        in_specs=[vmem] * 6,
        out_specs=(vmem,) * 6,
        name="scale",
    )(*resident(sums, *levels))


def to_next(face, *axes):
    sizes = [lax.axis_size(axis) for axis in axes]
    route = []
    for source in range(math.prod(sizes)):
        target, rest, scale = 0, source, 1
        for size in reversed(sizes):
            target += (rest % size + 1) % size * scale
            rest //= size
            scale *= size
        route.append((source, target))
    return lax.ppermute(face, sum(axes, ()), route)


def per_device(residual_in):
    devices = lax.axis_size(GX_GY_GZ)
    high, highs, xface = high_half(residual_in)
    xin = to_next(xface, GX)
    first, rest, yface, zface = low_half(residual_in, high, highs)
    yface, zface, edge = add_edges(xin, yface, zface)
    yin, zin, edgein = to_next(yface, GY), to_next(zface, GZ), to_next(edge, GY, GZ)
    *levels, sums = finish_levels(first, rest, xin, yin, zin, edgein, devices)
    sums = lax.all_to_all(sums, GX_GY_GZ, 0, 0, tiled=True)
    return tuple(scale_levels(sums, levels))


def solution(mesh):
    torus = Mesh(
        mesh.devices.reshape(mesh.shape["gx"], mesh.shape["gy"] // 2, 2, mesh.shape["gz"]), GX_GY_GZ
    )
    placed = P("gx", GY, "gz")
    return jax.shard_map(
        per_device,
        mesh=torus,
        in_specs=(placed,),
        out_specs=(placed,) * LEVELS + (P(),),
        check_vma=False,
    )
```

```python
import math

import jax
import jax.numpy as jnp
from jax import lax
from jax.experimental import pallas as pl
from jax.experimental.pallas import tpu as pltpu
from jax.sharding import Mesh
from jax.sharding import PartitionSpec as P

LEVELS = 5
GX = ("gx",)
GY = ("gy_0", "gy_1")
GZ = ("gz",)
GX_GY_GZ = ("gx", "gy_0", "gy_1", "gz")
EPSILON = 1e-06

BX, BY, BZ = 64, 64, 256
LANES = 128
CHUNK = 8
COUNT = [BX >> level for level in range(1, LEVELS + 1)]
ROWS = [40, 24, 16, 8, 8]
PASS_ROWS = [88, 56, 40, 24, 24]
REST_AT = [0, 0, 408, 552, 592]
REST_ROWS = 616
FIRST_ROWS = (COUNT[0] + 1) * ROWS[0]
HIGH_PLANES = [17, 8, 4, 2, 1]
LOW_PLANES = [17, 9, 5, 3, 2]
LANE_AT = [0, 0, 64, 96, 112]
LANE_COUNT = [128, 64, 32, 16, 8]
END_AT = 120
SPARE = 125
FACE_AT = [-1, 30, 45, 52, 55]


def face_lane(level, plane):
    return END_AT + level if plane == 0 else FACE_AT[level] + plane


def iota(shape, dim):
    return lax.broadcasted_iota(jnp.int32, shape, dim)


def tile_mask(level, shape):
    lane = iota(shape, len(shape) - 1)
    return (lane >= LANE_AT[level]) & (lane < LANE_AT[level] + LANE_COUNT[level])


def face_mask(level, shape):
    lane = iota(shape, len(shape) - 1)
    first = FACE_AT[level] + 1
    return (lane == END_AT + level) | ((lane >= first) & (lane < first + COUNT[level] - 1))


def stencil_table():
    lane = iota((1, BZ), 1)
    width = jnp.zeros((1, BZ), jnp.float32)
    centre = jnp.zeros((1, BZ), jnp.float32)
    scale = jnp.zeros((1, BZ), jnp.float32)
    for level in range(LEVELS):
        step = 2 << level
        base = LANE_AT[level] + (LANES if level else 0)
        inside = (lane >= base) & (lane < base + LANE_COUNT[level])
        past = lane == LANES + END_AT + level
        width = jnp.where(inside | past, float(step), width)
        scale = jnp.where(inside | past, 1.0 / 64 ** (level + 1), scale)
        centre = jnp.where(inside, ((lane - base) * step).astype(jnp.float32), centre)
        centre = jnp.where(past, float(BZ), centre)
    row = iota((BZ, BZ), 0).astype(jnp.float32)
    return (jnp.maximum(width - jnp.abs(row - centre), 0.0) * scale).astype(jnp.bfloat16)


def apply_table(values, table):
    high = values.astype(jnp.bfloat16)
    low = (values - high.astype(jnp.float32)).astype(jnp.bfloat16)
    top = jnp.dot(high, table, preferred_element_type=jnp.float32)
    return top + jnp.dot(low, table, preferred_element_type=jnp.float32)


def aligned(start):
    return start if isinstance(start, int) else pl.multiple_of(start, 8)


def y_pass(pass_ref, plane, level):
    base = aligned(plane * PASS_ROWS[level]) + 8
    full = (COUNT[level] // 8) * 8
    parts = []
    if full:
        middle = pass_ref[pl.ds(base, full, stride=2), :]
        after = pass_ref[pl.ds(base + 1, full, stride=2), :]
        before = pass_ref[pl.ds(base - 1, full, stride=2), :]
        parts.append(before + after + (middle + middle))
    rest = ROWS[level] - full
    before = pass_ref[pl.ds(base + 2 * full - 1, rest, stride=2), :]
    if level:
        middle = pass_ref[pl.ds(base + 2 * full, rest, stride=2), :]
        before += middle + middle
    if not full:
        before += pass_ref[pl.ds(base + 1, rest, stride=2), :]
    parts.append(before)
    return parts[0] if len(parts) == 1 else jnp.concatenate(parts, axis=0)


def high_from(level):
    return COUNT[level] // 2 + 1


def pass_scratch(planes):
    shapes = [(count * PASS_ROWS[level], LANES) for level, count in enumerate(planes)]
    return [pltpu.VMEM(shape, jnp.float32) for shape in shapes for _ in range(2)]


def clear_rims(pass_refs, planes):
    for level in range(LEVELS):
        body = BY if level == 0 else ROWS[level - 1]
        tail = PASS_ROWS[level] - 8 - body
        for ref in pass_refs[2 * level : 2 * level + 2]:
            for plane in range(planes[level]):
                base = plane * PASS_ROWS[level]
                ref[pl.ds(base, 8), :] = jnp.zeros((8, LANES), jnp.float32)
                if tail:
                    ref[pl.ds(base + 8 + body, tail), :] = jnp.zeros((tail, LANES), jnp.float32)


def first_planes(block_ref, pass_refs, plane_ref, planes, offset):
    for plane in planes:
        for half in range(2):
            lanes = slice(half * LANES, (half + 1) * LANES)
            before = block_ref[2 * plane, :, lanes]
            middle = block_ref[2 * plane + 1, :, lanes]
            after = block_ref[2 * plane + 2, :, lanes]
            pass_refs[half][pl.ds(aligned(plane * PASS_ROWS[0]) + 8, BY), :] = (
                before + after + (middle + middle)
            )
    for plane in planes:
        first_y(pass_refs, plane_ref, plane, offset)


def first_y(pass_refs, plane_ref, plane, offset):
    for half in range(2):
        lanes = slice(half * LANES, (half + 1) * LANES)
        at = aligned((plane + offset) * ROWS[0])
        plane_ref[pl.ds(at, ROWS[0]), lanes] = y_pass(pass_refs[half], plane, 0)


def later_planes(level, planes, load, pass_refs, stack_ref):
    for half in range(2):
        lanes = slice(half * LANES, (half + 1) * LANES)
        ref = pass_refs[2 * level + half]
        for local, plane in enumerate(planes):
            middle = load(2 * plane, lanes)
            total = middle + middle
            if plane > 0:
                total += load(2 * plane - 1, lanes)
            if plane < COUNT[level]:
                total += load(2 * plane + 1, lanes)
            ref[pl.ds(local * PASS_ROWS[level] + 8, ROWS[level - 1]), :] = total
        for local, plane in enumerate(planes):
            at = REST_AT[level] + plane * ROWS[level]
            stack_ref[pl.ds(at, ROWS[level]), lanes] = y_pass(ref, local, level)


def high_kernel(grid_ref, plane_ref, stack_ref, xface_ref, block_ref, sems, *pass_refs):
    half_x = BX // 2
    chunks = half_x // CHUNK

    def chunk_copy(index):
        return pltpu.make_async_copy(
            grid_ref.at[pl.ds(half_x + index * CHUNK, CHUNK)],
            block_ref.at[pl.ds(index * CHUNK + 1, CHUNK)],
            sems.at[index],
        )

    for index in range(chunks):
        chunk_copy(index).start()
    table = stencil_table()
    block_ref[0] = jnp.zeros((BY, BZ), jnp.float32)
    clear_rims(pass_refs, HIGH_PLANES)

    def step(index, carry):
        chunk_copy(index).wait()
        planes = [index * (CHUNK // 2) + part for part in range(CHUNK // 2)]
        first_planes(block_ref, pass_refs, plane_ref, planes, COUNT[0] // 2)
        return carry

    lax.fori_loop(0, chunks, step, 0)
    for half in range(2):
        lanes = slice(half * LANES, (half + 1) * LANES)
        at = COUNT[0] // 2 * PASS_ROWS[0] + 8
        pass_refs[half][pl.ds(at, BY), :] = block_ref[half_x, :, lanes]
    first_y(pass_refs, plane_ref, COUNT[0] // 2, COUNT[0] // 2)
    for level in range(1, LEVELS):

        def load(plane, lanes, level=level):
            source = plane_ref if level == 1 else stack_ref
            at = (REST_AT[level - 1] if level > 1 else 0) + plane * ROWS[level - 1]
            return source[pl.ds(at, ROWS[level - 1]), lanes]

        later_planes(level, range(high_from(level), COUNT[level] + 1), load, pass_refs, stack_ref)

    keep_x = sends(GX)
    parts = [plane_ref[pl.ds(COUNT[0] * ROWS[0], ROWS[0]), :]]
    for level in range(1, LEVELS):
        parts.append(stack_ref[pl.ds(REST_AT[level] + COUNT[level] * ROWS[level], ROWS[level]), :])
    faces = apply_table(jnp.concatenate(parts, axis=0), table) * keep_x
    tiles = [jnp.where(iota((ROWS[0], LANES), 1) == END_AT, faces[: ROWS[0], LANES:], 0.0)]
    at = ROWS[0]
    for level in range(1, LEVELS):
        shape = (ROWS[level], LANES)
        keep = tile_mask(level, shape) | (iota(shape, 1) == END_AT + level)
        face = jnp.where(keep, faces[at : at + ROWS[level], LANES:], 0.0)
        at += ROWS[level]
        if ROWS[level] < ROWS[0]:
            blank = jnp.zeros((ROWS[0] - ROWS[level], LANES), jnp.float32)
            face = jnp.concatenate([face, blank], axis=0)
        tiles.append(face)
    tile = sum(tiles[1:], tiles[0])
    xface_ref[pl.ds(0, 32), :] = faces[:32, :LANES]
    lane = iota((16, LANES), 1)
    spare = pltpu.roll(jnp.where(lane == END_AT, tile[16:32], 0.0), SPARE - END_AT, 1)
    xface_ref[pl.ds(32, 16), :] = tile[:16] + spare
    lane = iota((1, LANES), 1)
    row = iota((8, LANES), 0)
    second = jnp.where(lane == END_AT, tile[32:33], tile[16:17])
    xface_ref[pl.ds(48, 8), :] = jnp.where(
        row == 0, faces[32:33, :LANES], jnp.where(row == 1, second, 0.0)
    )


def high_half(block):
    f32 = jnp.float32
    vmem = pl.BlockSpec(memory_space=pltpu.VMEM)
    return pl.pallas_call(
        high_kernel,
        out_shape=(
            pltpu.VMEM((FIRST_ROWS, BZ), f32),
            pltpu.VMEM((REST_ROWS, BZ), f32),
            pltpu.VMEM((56, LANES), f32),
        ),
        in_specs=[pl.BlockSpec(memory_space=pl.ANY)],
        out_specs=(vmem,) * 3,
        scratch_shapes=[
            pltpu.VMEM((BX // 2 + 1, BY, BZ), f32),
            pltpu.SemaphoreType.DMA((BX // 2 // CHUNK,)),
        ]
        + pass_scratch(HIGH_PLANES),
        name="high_half",
    )(block)


def low_kernel(grid_ref, high_ref, highs_ref, first_ref, rest_ref, yface_ref, zface_ref, *scratch):
    block_ref, plane_ref, stack_ref, end_ref, sems = scratch[:5]
    pass_refs = scratch[5:]
    half_x = BX // 2
    chunks = half_x // CHUNK
    low = high_from(0)

    def copy(start, size, index):
        return pltpu.make_async_copy(
            grid_ref.at[pl.ds(start, size)], block_ref.at[pl.ds(start + 1, size)], sems.at[index]
        )

    for index in range(chunks):
        copy(index * CHUNK, CHUNK, index).start()
    copy(half_x, 2, chunks).start()
    table = stencil_table()
    block_ref[0] = jnp.zeros((BY, BZ), jnp.float32)
    clear_rims(pass_refs, LOW_PLANES)
    for level in range(1, LEVELS):
        at = REST_AT[level] + high_from(level) * ROWS[level]
        size = (COUNT[level] + 1 - high_from(level)) * ROWS[level]
        stack_ref[pl.ds(at, size), :] = highs_ref[pl.ds(at, size), :]

    def first_z(source, at, size):
        both = apply_table(source[pl.ds(at, size), :], table)
        first_ref[pl.ds(at, size), :] = both[:, :LANES]
        end_ref[pl.ds(at, size), :] = both[:, LANES:]

    def high_z(index, carry):
        span = 5 * ROWS[0]
        first_z(high_ref, aligned(low * ROWS[0] + index * span), span)
        return carry

    lax.fori_loop(0, (COUNT[0] - low) // 5, high_z, 0)

    def step(index, carry):
        copy(index * CHUNK, CHUNK, index).wait()
        planes = [index * (CHUNK // 2) + part for part in range(CHUNK // 2)]
        first_planes(block_ref, pass_refs, plane_ref, planes, 0)
        span = CHUNK // 2 * ROWS[0]
        first_z(plane_ref, aligned(index * span), span)
        return carry

    lax.fori_loop(0, chunks, step, 0)
    copy(half_x, 2, chunks).wait()
    first_planes(block_ref, pass_refs, plane_ref, [low - 1], 0)
    first_z(plane_ref, (low - 1) * ROWS[0], ROWS[0])
    for level in range(1, LEVELS):

        def load(plane, lanes, level=level):
            if level == 1:
                source = plane_ref if plane < low else high_ref
                return source[pl.ds(plane * ROWS[0], ROWS[0]), lanes]
            return stack_ref[pl.ds(REST_AT[level - 1] + plane * ROWS[level - 1], ROWS[level - 1]), lanes]

        later_planes(level, range(high_from(level)), load, pass_refs, stack_ref)
    rest_ref[...] = apply_table(stack_ref[...], table[:, LANES:])

    def right_rows(level, plane):
        ref = end_ref if level == 0 else rest_ref
        at = (0 if level == 0 else REST_AT[level]) + plane * ROWS[level]
        return ref[pl.ds(at, ROWS[level]), :]

    yface_ref[pl.ds(0, 32), :] = first_ref[pl.ds(COUNT[0], COUNT[0], stride=ROWS[0]), :]
    yface_ref[pl.ds(32, 16), :] = jnp.zeros((16, LANES), jnp.float32)
    for level in range(1, LEVELS):
        count = COUNT[level]
        at = REST_AT[level] + count
        if count >= 8:
            new = rest_ref[pl.ds(at, count, stride=ROWS[level]), :]
        else:
            new = jnp.zeros((8, LANES), jnp.float32)
            for plane in range(count):
                row = rest_ref[pl.ds(at + plane * ROWS[level], 1), :]
                new = jnp.where(iota((8, LANES), 0) == plane, row, new)
        size = max(count, 8)
        old = yface_ref[pl.ds(32, size), :]
        yface_ref[pl.ds(32, size), :] = jnp.where(tile_mask(level, (size, LANES)), new, old)

    for level in range(LEVELS):
        lane = iota((ROWS[level], LANES), 1)
        face = jnp.zeros((ROWS[level], LANES), jnp.float32)
        for plane in range(COUNT[level]):
            values = right_rows(level, plane)
            target = face_lane(level, plane)
            shift = (target - END_AT - level) % LANES
            if shift:
                values = pltpu.roll(values, shift, 1)
            face = jnp.where(lane == target, values, face)
        if level == 0:
            zface_ref[...] = face
        else:
            zface_ref[pl.ds(0, ROWS[level]), :] = zface_ref[pl.ds(0, ROWS[level]), :] + face


def low_half(block, high, highs):
    f32 = jnp.float32
    rows = COUNT[0] * ROWS[0]
    vmem = pl.BlockSpec(memory_space=pltpu.VMEM)
    return pl.pallas_call(
        low_kernel,
        out_shape=(
            pltpu.VMEM((rows, LANES), f32),
            pltpu.VMEM((REST_ROWS, LANES), f32),
            pltpu.VMEM((48, LANES), f32),
            pltpu.VMEM((ROWS[0], LANES), f32),
        ),
        in_specs=[pl.BlockSpec(memory_space=pl.ANY), vmem, vmem],
        out_specs=(vmem,) * 4,
        scratch_shapes=[
            pltpu.VMEM((BX // 2 + 3, BY, BZ), f32),
            pltpu.VMEM((high_from(0) * ROWS[0], BZ), f32),
            pltpu.VMEM((REST_ROWS, BZ), f32),
            pltpu.VMEM((rows, LANES), f32),
            pltpu.SemaphoreType.DMA((BX // 2 // CHUNK + 1,)),
        ]
        + pass_scratch(LOW_PLANES),
        name="low_half",
    )(block, *resident(high, highs))


def edge_kernel(xin_ref, yface_ref, zface_ref, yout_ref, zout_ref, yzout_ref):
    count = COUNT[0]
    keep_y = sends(GY)
    keep_z = sends(GZ)
    lane = iota((16, LANES), 1)
    top = xin_ref[pl.ds(32, 16), :]
    ends = (lane >= END_AT) & (lane < END_AT + LEVELS)
    spare = pltpu.roll(top, LANES + END_AT - SPARE, 1)
    second = xin_ref[pl.ds(49, 1), :]
    last = iota((1, LANES), 1)
    middle = jnp.where(lane == END_AT, spare, 0.0) + jnp.where(
        (iota((16, LANES), 0) == 0) & (lane == END_AT + 1), second, 0.0
    )
    bottom = jnp.where((iota((8, LANES), 0) == 0) & (last == END_AT), second, 0.0)
    zface = zface_ref[...] + jnp.concatenate([jnp.where(ends, top, 0.0), middle, bottom], axis=0)
    zout_ref[...] = zface[:count] * keep_z
    edge = jnp.zeros((1, LANES), jnp.float32)
    corner = jnp.zeros((1, LANES), jnp.float32)
    for level in range(LEVELS):
        at = COUNT[level]
        if level:
            source = second if level == 1 else top[at : at + 1]
            edge = jnp.where(tile_mask(level, (1, LANES)), source, edge)
        corner = jnp.where(face_mask(level, (1, LANES)), zface[at : at + 1], corner)
    added = jnp.where(iota((count, LANES), 0) == 0, xin_ref[pl.ds(48, 1), :], 0.0)
    yout_ref[pl.ds(0, count), :] = (yface_ref[pl.ds(0, count), :] + added) * keep_y
    added = jnp.where(iota((16, LANES), 0) == 0, edge, 0.0)
    yout_ref[pl.ds(count, 16), :] = (yface_ref[pl.ds(count, 16), :] + added) * keep_y
    yzout_ref[...] = jnp.where(iota((8, LANES), 0) == 0, corner, 0.0) * (keep_y * keep_z)


def sends(axis):
    index = 0
    for name in axis:
        index = index * lax.axis_size(name) + lax.axis_index(name)
    return jnp.where(index < lax.axis_size(axis) - 1, 1.0, 0.0)


def resident(*arrays):
    return [pltpu.with_memory_space_constraint(array, pltpu.VMEM) for array in arrays]


def add_edges(xin, yface, zface):
    f32 = jnp.float32
    vmem = pl.BlockSpec(memory_space=pltpu.VMEM)
    return pl.pallas_call(
        edge_kernel,
        out_shape=(
            pltpu.VMEM((48, LANES), f32),
            pltpu.VMEM((COUNT[0], LANES), f32),
            pltpu.VMEM((8, LANES), f32),
        ),
        in_specs=[vmem] * 3,
        out_specs=(vmem,) * 3,
        name="edges",
    )(*resident(xin, yface, zface))


def finish_kernel(first_ref, rest_ref, xin_ref, yin_ref, zin_ref, yzin_ref, *out_refs):
    sums_ref = out_refs[LEVELS]
    corner = yzin_ref[...]
    zface = jnp.concatenate([zin_ref[pl.ds(0, 8), :] + corner, zin_ref[pl.ds(8, COUNT[0] - 8), :]], axis=0)
    sums = jnp.zeros((1, LANES), jnp.float32)
    for level in range(LEVELS):
        count = COUNT[level]
        rows = max(count, 8)
        face_at = 32 if level else 0
        source = first_ref if level == 0 else rest_ref
        shape = (rows, LANES)
        inside = tile_mask(level, shape) & (iota(shape, 0) < count)
        zlane = iota(shape, 1) == LANE_AT[level]
        squares = jnp.zeros((8, LANES), jnp.float32)
        for plane in range(count):
            at = REST_AT[level] + plane * ROWS[level]
            values = source[pl.ds(at, rows), :]
            if plane == 0:
                values = values + xin_ref[pl.ds(face_at, rows), :]
            yrow = jnp.where(iota((8, LANES), 0) == 0, yin_ref[pl.ds(face_at + plane, 1), :], 0.0)
            if rows > 8:
                yrow = jnp.concatenate([yrow, jnp.zeros((rows - 8, LANES), jnp.float32)], axis=0)
            shift = (LANE_AT[level] - face_lane(level, plane)) % LANES
            zcol = zface[:rows]
            if shift:
                zcol = pltpu.roll(zcol, shift, 1)
            values = values + yrow + jnp.where(zlane, zcol, 0.0)
            if level:
                values = jnp.where(inside, values, 0.0)
            out_refs[level][plane] = values
            squared = values * values
            for tile in range(rows // 8):
                squares = squares + squared[tile * 8 : tile * 8 + 8]
        total = jnp.sum(jnp.sum(squares, axis=0, keepdims=True), axis=1, keepdims=True)
        sums = jnp.where(iota((1, LANES), 1) == level, total, sums)
    sums_ref[...] = jnp.broadcast_to(sums, sums_ref.shape)


def finish_levels(first, rest, xin, yin, zin, yzin, devices):
    f32 = jnp.float32
    vmem = pl.BlockSpec(memory_space=pltpu.VMEM)
    shapes = [(COUNT[level], max(COUNT[level], 8), LANES) for level in range(LEVELS)]
    shapes.append((devices, LANES))
    return pl.pallas_call(
        finish_kernel,
        out_shape=tuple(pltpu.VMEM(shape, f32) for shape in shapes),
        in_specs=[vmem] * 6,
        out_specs=(vmem,) * 6,
        name="finish",
    )(*resident(first, rest, xin, yin, zin, yzin))


def scale_kernel(sums_ref, *refs):
    level_refs = refs[:LEVELS]
    out_refs = refs[LEVELS : 2 * LEVELS]
    scales_ref = refs[2 * LEVELS]
    devices = sums_ref.shape[0]
    totals = jnp.sum(sums_ref[...], axis=0, keepdims=True)
    lane = iota((1, LANES), 1)
    product = jnp.ones((1, 1), jnp.float32)
    scales = jnp.zeros((1, LANES), jnp.float32)
    for level in range(LEVELS):
        cells = COUNT[level] * COUNT[level] * LANE_COUNT[level] * devices
        total = jnp.sum(jnp.where(lane == level, totals, 0.0), axis=1, keepdims=True)
        scale = jnp.sqrt(total / (product * product) * (1.0 / cells) + EPSILON)
        product = product * scale
        scales = jnp.where(lane == level, scale, scales)
        factor = jnp.broadcast_to(1.0 / product, (8, LANES))
        count = COUNT[level]
        for plane in range(count):
            for tile in range(max(count // 8, 1)):
                values = level_refs[level][plane, pl.ds(tile * 8, 8), :] * factor
                if LANE_AT[level]:
                    values = pltpu.roll(values, LANES - LANE_AT[level], 1)
                size = min(count, 8)
                out_refs[level][plane, pl.ds(tile * 8, size), :] = values[:size, : LANE_COUNT[level]]
    scales_ref[...] = scales[0, :LEVELS]


def scale_levels(sums, levels):
    f32 = jnp.float32
    vmem = pl.BlockSpec(memory_space=pltpu.VMEM)
    shapes = [(COUNT[level], COUNT[level], LANE_COUNT[level]) for level in range(LEVELS)]
    shapes.append((LEVELS,))
    return pl.pallas_call(
        scale_kernel,
        out_shape=tuple(jax.ShapeDtypeStruct(shape, f32) for shape in shapes),
        in_specs=[vmem] * 6,
        out_specs=(vmem,) * 6,
        name="scale",
    )(*resident(sums, *levels))


def to_next(face, *axes):
    sizes = [lax.axis_size(axis) for axis in axes]
    route = []
    for source in range(math.prod(sizes)):
        target, rest, scale = 0, source, 1
        for size in reversed(sizes):
            target += (rest % size + 1) % size * scale
            rest //= size
            scale *= size
        route.append((source, target))
    return lax.ppermute(face, sum(axes, ()), route)


def per_device(residual_in):
    devices = lax.axis_size(GX_GY_GZ)
    high, highs, xface = high_half(residual_in)
    xin = to_next(xface, GX)
    first, rest, yface, zface = low_half(residual_in, high, highs)
    yface, zface, edge = add_edges(xin, yface, zface)
    edgein = to_next(edge, GY, GZ)
    zin = to_next(zface, GZ)
    yin = to_next(yface, GY)
    *levels, sums = finish_levels(first, rest, xin, yin, zin, edgein, devices)
    sums = lax.all_to_all(sums, GX_GY_GZ, 0, 0, tiled=True)
    return tuple(scale_levels(sums, levels))


def solution(mesh):
    torus = Mesh(
        mesh.devices.reshape(mesh.shape["gx"], mesh.shape["gy"] // 2, 2, mesh.shape["gz"]), GX_GY_GZ
    )
    placed = P("gx", GY, "gz")
    return jax.shard_map(
        per_device,
        mesh=torus,
        in_specs=(placed,),
        out_specs=(placed,) * LEVELS + (P(),),
        check_vma=False,
    )
```

```python
import math

import jax
import jax.numpy as jnp
from jax import lax
from jax.experimental import pallas as pl
from jax.experimental.pallas import tpu as pltpu
from jax.sharding import Mesh
from jax.sharding import PartitionSpec as P

LEVELS = 5
GX = ("gx",)
GY = ("gy_0", "gy_1")
GZ = ("gz",)
GX_GY_GZ = ("gx", "gy_0", "gy_1", "gz")
EPSILON = 1e-06

BX, BY, BZ = 64, 64, 256
LANES = 128
CHUNK = 8
LOW_CHUNK = 16
COUNT = [BX >> level for level in range(1, LEVELS + 1)]
ROWS = [40, 24, 16, 8, 8]
PASS_ROWS = [88, 56, 40, 24, 24]
REST_AT = [0, 0, 408, 552, 592]
REST_ROWS = 616
FIRST_ROWS = (COUNT[0] + 1) * ROWS[0]
HIGH_PLANES = [17, 8, 4, 2, 1]
LOW_PLANES = [17, 9, 5, 3, 2]
LANE_AT = [0, 0, 64, 96, 112]
LANE_COUNT = [128, 64, 32, 16, 8]
END_AT = 120
SPARE = 125
FACE_AT = [-1, 30, 45, 52, 55]


def face_lane(level, plane):
    return END_AT + level if plane == 0 else FACE_AT[level] + plane


def iota(shape, dim):
    return lax.broadcasted_iota(jnp.int32, shape, dim)


def tile_mask(level, shape):
    lane = iota(shape, len(shape) - 1)
    return (lane >= LANE_AT[level]) & (lane < LANE_AT[level] + LANE_COUNT[level])


def face_mask(level, shape):
    lane = iota(shape, len(shape) - 1)
    first = FACE_AT[level] + 1
    return (lane == END_AT + level) | ((lane >= first) & (lane < first + COUNT[level] - 1))


def stencil_table():
    lane = iota((1, BZ), 1)
    width = jnp.zeros((1, BZ), jnp.float32)
    centre = jnp.zeros((1, BZ), jnp.float32)
    scale = jnp.zeros((1, BZ), jnp.float32)
    for level in range(LEVELS):
        step = 2 << level
        base = LANE_AT[level] + (LANES if level else 0)
        inside = (lane >= base) & (lane < base + LANE_COUNT[level])
        past = lane == LANES + END_AT + level
        width = jnp.where(inside | past, float(step), width)
        scale = jnp.where(inside | past, 1.0 / 64 ** (level + 1), scale)
        centre = jnp.where(inside, ((lane - base) * step).astype(jnp.float32), centre)
        centre = jnp.where(past, float(BZ), centre)
    row = iota((BZ, BZ), 0).astype(jnp.float32)
    return (jnp.maximum(width - jnp.abs(row - centre), 0.0) * scale).astype(jnp.bfloat16)


def apply_table(values, table):
    left = values - values.astype(jnp.bfloat16).astype(jnp.float32)
    both = jnp.concatenate([values, left], axis=0).astype(jnp.bfloat16)
    out = jnp.dot(both, table, preferred_element_type=jnp.float32)
    return out[: values.shape[0]] + out[values.shape[0] :]


def aligned(start):
    return start if isinstance(start, int) else pl.multiple_of(start, 8)


def y_pass(pass_ref, plane, level):
    base = aligned(plane * PASS_ROWS[level]) + 8
    full = (COUNT[level] // 8) * 8
    parts = []
    if full:
        middle = pass_ref[pl.ds(base, full, stride=2), :]
        after = pass_ref[pl.ds(base + 1, full, stride=2), :]
        before = pass_ref[pl.ds(base - 1, full, stride=2), :]
        parts.append(before + after + (middle + middle))
    rest = ROWS[level] - full
    before = pass_ref[pl.ds(base + 2 * full - 1, rest, stride=2), :]
    if level:
        middle = pass_ref[pl.ds(base + 2 * full, rest, stride=2), :]
        before += middle + middle
    if not full:
        before += pass_ref[pl.ds(base + 1, rest, stride=2), :]
    parts.append(before)
    return parts[0] if len(parts) == 1 else jnp.concatenate(parts, axis=0)


def high_from(level):
    return COUNT[level] // 2 + 1


def pass_scratch(planes):
    shapes = [(count * PASS_ROWS[level], LANES) for level, count in enumerate(planes)]
    return [pltpu.VMEM(shape, jnp.float32) for shape in shapes for _ in range(2)]


def clear_rims(pass_refs, planes):
    for level in range(LEVELS):
        body = BY if level == 0 else ROWS[level - 1]
        tail = PASS_ROWS[level] - 8 - body
        for ref in pass_refs[2 * level : 2 * level + 2]:
            for plane in range(planes[level]):
                base = plane * PASS_ROWS[level]
                ref[pl.ds(base, 8), :] = jnp.zeros((8, LANES), jnp.float32)
                if tail:
                    ref[pl.ds(base + 8 + body, tail), :] = jnp.zeros((tail, LANES), jnp.float32)


def first_planes(block_ref, pass_refs, plane_ref, planes, offset):
    for plane in planes:
        for half in range(2):
            lanes = slice(half * LANES, (half + 1) * LANES)
            before = block_ref[2 * plane, :, lanes]
            middle = block_ref[2 * plane + 1, :, lanes]
            after = block_ref[2 * plane + 2, :, lanes]
            pass_refs[half][pl.ds(aligned(plane * PASS_ROWS[0]) + 8, BY), :] = (
                before + after + (middle + middle)
            )
    for plane in planes:
        first_y(pass_refs, plane_ref, plane, offset)


def first_y(pass_refs, plane_ref, plane, offset):
    for half in range(2):
        lanes = slice(half * LANES, (half + 1) * LANES)
        at = aligned((plane + offset) * ROWS[0])
        plane_ref[pl.ds(at, ROWS[0]), lanes] = y_pass(pass_refs[half], plane, 0)


def later_planes(level, planes, load, pass_refs, stack_ref):
    for half in range(2):
        lanes = slice(half * LANES, (half + 1) * LANES)
        ref = pass_refs[2 * level + half]
        for local, plane in enumerate(planes):
            middle = load(2 * plane, lanes)
            total = middle + middle
            if plane > 0:
                total += load(2 * plane - 1, lanes)
            if plane < COUNT[level]:
                total += load(2 * plane + 1, lanes)
            ref[pl.ds(local * PASS_ROWS[level] + 8, ROWS[level - 1]), :] = total
        for local, plane in enumerate(planes):
            at = REST_AT[level] + plane * ROWS[level]
            stack_ref[pl.ds(at, ROWS[level]), lanes] = y_pass(ref, local, level)


def high_kernel(grid_ref, plane_ref, stack_ref, xface_ref, block_ref, sems, *pass_refs):
    half_x = BX // 2
    chunks = half_x // CHUNK

    def chunk_copy(index):
        return pltpu.make_async_copy(
            grid_ref.at[pl.ds(half_x + index * CHUNK, CHUNK)],
            block_ref.at[pl.ds(index * CHUNK + 1, CHUNK)],
            sems.at[index],
        )

    for index in range(chunks):
        chunk_copy(index).start()
    table = stencil_table()
    block_ref[0] = jnp.zeros((BY, BZ), jnp.float32)
    clear_rims(pass_refs, HIGH_PLANES)

    def step(index, carry):
        chunk_copy(index).wait()
        planes = [index * (CHUNK // 2) + part for part in range(CHUNK // 2)]
        first_planes(block_ref, pass_refs, plane_ref, planes, COUNT[0] // 2)
        return carry

    lax.fori_loop(0, chunks, step, 0)
    for half in range(2):
        lanes = slice(half * LANES, (half + 1) * LANES)
        at = COUNT[0] // 2 * PASS_ROWS[0] + 8
        pass_refs[half][pl.ds(at, BY), :] = block_ref[half_x, :, lanes]
    first_y(pass_refs, plane_ref, COUNT[0] // 2, COUNT[0] // 2)
    for level in range(1, LEVELS):

        def load(plane, lanes, level=level):
            source = plane_ref if level == 1 else stack_ref
            at = (REST_AT[level - 1] if level > 1 else 0) + plane * ROWS[level - 1]
            return source[pl.ds(at, ROWS[level - 1]), lanes]

        later_planes(level, range(high_from(level), COUNT[level] + 1), load, pass_refs, stack_ref)

    keep_x = sends(GX)
    parts = [plane_ref[pl.ds(COUNT[0] * ROWS[0], ROWS[0]), :]]
    for level in range(1, LEVELS):
        parts.append(stack_ref[pl.ds(REST_AT[level] + COUNT[level] * ROWS[level], ROWS[level]), :])
    faces = apply_table(jnp.concatenate(parts, axis=0), table) * keep_x
    tiles = [jnp.where(iota((ROWS[0], LANES), 1) == END_AT, faces[: ROWS[0], LANES:], 0.0)]
    at = ROWS[0]
    for level in range(1, LEVELS):
        shape = (ROWS[level], LANES)
        keep = tile_mask(level, shape) | (iota(shape, 1) == END_AT + level)
        face = jnp.where(keep, faces[at : at + ROWS[level], LANES:], 0.0)
        at += ROWS[level]
        if ROWS[level] < ROWS[0]:
            blank = jnp.zeros((ROWS[0] - ROWS[level], LANES), jnp.float32)
            face = jnp.concatenate([face, blank], axis=0)
        tiles.append(face)
    tile = sum(tiles[1:], tiles[0])
    xface_ref[pl.ds(0, 32), :] = faces[:32, :LANES]
    lane = iota((16, LANES), 1)
    spare = pltpu.roll(jnp.where(lane == END_AT, tile[16:32], 0.0), SPARE - END_AT, 1)
    xface_ref[pl.ds(32, 16), :] = tile[:16] + spare
    lane = iota((1, LANES), 1)
    row = iota((8, LANES), 0)
    second = jnp.where(lane == END_AT, tile[32:33], tile[16:17])
    xface_ref[pl.ds(48, 8), :] = jnp.where(
        row == 0, faces[32:33, :LANES], jnp.where(row == 1, second, 0.0)
    )


def high_half(block):
    f32 = jnp.float32
    vmem = pl.BlockSpec(memory_space=pltpu.VMEM)
    return pl.pallas_call(
        high_kernel,
        out_shape=(
            pltpu.VMEM((FIRST_ROWS, BZ), f32),
            pltpu.VMEM((REST_ROWS, BZ), f32),
            pltpu.VMEM((56, LANES), f32),
        ),
        in_specs=[pl.BlockSpec(memory_space=pl.ANY)],
        out_specs=(vmem,) * 3,
        scratch_shapes=[
            pltpu.VMEM((BX // 2 + 1, BY, BZ), f32),
            pltpu.SemaphoreType.DMA((BX // 2 // CHUNK,)),
        ]
        + pass_scratch(HIGH_PLANES),
        name="high_half",
    )(block)


def low_kernel(grid_ref, high_ref, highs_ref, first_ref, rest_ref, yface_ref, zface_ref, *scratch):
    block_ref, plane_ref, stack_ref, end_ref, sems = scratch[:5]
    pass_refs = scratch[5:]
    half_x = BX // 2
    chunks = half_x // LOW_CHUNK
    low = high_from(0)

    def copy(start, size, index):
        return pltpu.make_async_copy(
            grid_ref.at[pl.ds(start, size)], block_ref.at[pl.ds(start + 1, size)], sems.at[index]
        )

    for index in range(chunks):
        copy(index * LOW_CHUNK, LOW_CHUNK, index).start()
    copy(half_x, 2, chunks).start()
    table = stencil_table()
    block_ref[0] = jnp.zeros((BY, BZ), jnp.float32)
    clear_rims(pass_refs, LOW_PLANES)
    for level in range(1, LEVELS):
        at = REST_AT[level] + high_from(level) * ROWS[level]
        size = (COUNT[level] + 1 - high_from(level)) * ROWS[level]
        stack_ref[pl.ds(at, size), :] = highs_ref[pl.ds(at, size), :]

    def first_z(source, at, size):
        both = apply_table(source[pl.ds(at, size), :], table)
        first_ref[pl.ds(at, size), :] = both[:, :LANES]
        end_ref[pl.ds(at, size), :] = both[:, LANES:]

    def high_z(index, carry):
        span = 5 * ROWS[0]
        first_z(high_ref, aligned(low * ROWS[0] + index * span), span)
        return carry

    lax.fori_loop(0, (COUNT[0] - low) // 5, high_z, 0)

    def step(index, carry):
        copy(index * LOW_CHUNK, LOW_CHUNK, index).wait()
        planes = [index * (LOW_CHUNK // 2) + part for part in range(LOW_CHUNK // 2)]
        first_planes(block_ref, pass_refs, plane_ref, planes, 0)
        span = LOW_CHUNK // 2 * ROWS[0]
        first_z(plane_ref, aligned(index * span), span)
        return carry

    lax.fori_loop(0, chunks, step, 0)
    copy(half_x, 2, chunks).wait()
    first_planes(block_ref, pass_refs, plane_ref, [low - 1], 0)
    first_z(plane_ref, (low - 1) * ROWS[0], ROWS[0])
    for level in range(1, LEVELS):

        def load(plane, lanes, level=level):
            if level == 1:
                source = plane_ref if plane < low else high_ref
                return source[pl.ds(plane * ROWS[0], ROWS[0]), lanes]
            return stack_ref[pl.ds(REST_AT[level - 1] + plane * ROWS[level - 1], ROWS[level - 1]), lanes]

        later_planes(level, range(high_from(level)), load, pass_refs, stack_ref)
    rest_ref[...] = apply_table(stack_ref[...], table[:, LANES:])

    def right_rows(level, plane):
        ref = end_ref if level == 0 else rest_ref
        at = (0 if level == 0 else REST_AT[level]) + plane * ROWS[level]
        return ref[pl.ds(at, ROWS[level]), :]

    yface_ref[pl.ds(0, 32), :] = first_ref[pl.ds(COUNT[0], COUNT[0], stride=ROWS[0]), :]
    yface_ref[pl.ds(32, 16), :] = jnp.zeros((16, LANES), jnp.float32)
    for level in range(1, LEVELS):
        count = COUNT[level]
        at = REST_AT[level] + count
        if count >= 8:
            new = rest_ref[pl.ds(at, count, stride=ROWS[level]), :]
        else:
            new = jnp.zeros((8, LANES), jnp.float32)
            for plane in range(count):
                row = rest_ref[pl.ds(at + plane * ROWS[level], 1), :]
                new = jnp.where(iota((8, LANES), 0) == plane, row, new)
        size = max(count, 8)
        old = yface_ref[pl.ds(32, size), :]
        yface_ref[pl.ds(32, size), :] = jnp.where(tile_mask(level, (size, LANES)), new, old)

    for level in range(LEVELS):
        lane = iota((ROWS[level], LANES), 1)
        face = jnp.zeros((ROWS[level], LANES), jnp.float32)
        for plane in range(COUNT[level]):
            values = right_rows(level, plane)
            target = face_lane(level, plane)
            shift = (target - END_AT - level) % LANES
            if shift:
                values = pltpu.roll(values, shift, 1)
            face = jnp.where(lane == target, values, face)
        if level == 0:
            zface_ref[...] = face
        else:
            zface_ref[pl.ds(0, ROWS[level]), :] = zface_ref[pl.ds(0, ROWS[level]), :] + face


def low_half(block, high, highs):
    f32 = jnp.float32
    rows = COUNT[0] * ROWS[0]
    vmem = pl.BlockSpec(memory_space=pltpu.VMEM)
    return pl.pallas_call(
        low_kernel,
        out_shape=(
            pltpu.VMEM((rows, LANES), f32),
            pltpu.VMEM((REST_ROWS, LANES), f32),
            pltpu.VMEM((48, LANES), f32),
            pltpu.VMEM((ROWS[0], LANES), f32),
        ),
        in_specs=[pl.BlockSpec(memory_space=pl.ANY), vmem, vmem],
        out_specs=(vmem,) * 4,
        scratch_shapes=[
            pltpu.VMEM((BX // 2 + 3, BY, BZ), f32),
            pltpu.VMEM((high_from(0) * ROWS[0], BZ), f32),
            pltpu.VMEM((REST_ROWS, BZ), f32),
            pltpu.VMEM((rows, LANES), f32),
            pltpu.SemaphoreType.DMA((BX // 2 // LOW_CHUNK + 1,)),
        ]
        + pass_scratch(LOW_PLANES),
        name="low_half",
    )(block, *resident(high, highs))


def edge_kernel(xin_ref, yface_ref, zface_ref, yout_ref, zout_ref, yzout_ref):
    count = COUNT[0]
    keep_y = sends(GY)
    keep_z = sends(GZ)
    lane = iota((16, LANES), 1)
    top = xin_ref[pl.ds(32, 16), :]
    ends = (lane >= END_AT) & (lane < END_AT + LEVELS)
    spare = pltpu.roll(top, LANES + END_AT - SPARE, 1)
    second = xin_ref[pl.ds(49, 1), :]
    last = iota((1, LANES), 1)
    middle = jnp.where(lane == END_AT, spare, 0.0) + jnp.where(
        (iota((16, LANES), 0) == 0) & (lane == END_AT + 1), second, 0.0
    )
    bottom = jnp.where((iota((8, LANES), 0) == 0) & (last == END_AT), second, 0.0)
    zface = zface_ref[...] + jnp.concatenate([jnp.where(ends, top, 0.0), middle, bottom], axis=0)
    zout_ref[...] = zface[:count] * keep_z
    edge = jnp.zeros((1, LANES), jnp.float32)
    corner = jnp.zeros((1, LANES), jnp.float32)
    for level in range(LEVELS):
        at = COUNT[level]
        if level:
            source = second if level == 1 else top[at : at + 1]
            edge = jnp.where(tile_mask(level, (1, LANES)), source, edge)
        corner = jnp.where(face_mask(level, (1, LANES)), zface[at : at + 1], corner)
    added = jnp.where(iota((count, LANES), 0) == 0, xin_ref[pl.ds(48, 1), :], 0.0)
    yout_ref[pl.ds(0, count), :] = (yface_ref[pl.ds(0, count), :] + added) * keep_y
    added = jnp.where(iota((16, LANES), 0) == 0, edge, 0.0)
    yout_ref[pl.ds(count, 16), :] = (yface_ref[pl.ds(count, 16), :] + added) * keep_y
    yzout_ref[...] = jnp.where(iota((8, LANES), 0) == 0, corner, 0.0) * (keep_y * keep_z)


def sends(axis):
    index = 0
    for name in axis:
        index = index * lax.axis_size(name) + lax.axis_index(name)
    return jnp.where(index < lax.axis_size(axis) - 1, 1.0, 0.0)


def resident(*arrays):
    return [pltpu.with_memory_space_constraint(array, pltpu.VMEM) for array in arrays]


def add_edges(xin, yface, zface):
    f32 = jnp.float32
    vmem = pl.BlockSpec(memory_space=pltpu.VMEM)
    return pl.pallas_call(
        edge_kernel,
        out_shape=(
            pltpu.VMEM((48, LANES), f32),
            pltpu.VMEM((COUNT[0], LANES), f32),
            pltpu.VMEM((8, LANES), f32),
        ),
        in_specs=[vmem] * 3,
        out_specs=(vmem,) * 3,
        name="edges",
    )(*resident(xin, yface, zface))


def finish_kernel(first_ref, rest_ref, xin_ref, yin_ref, zin_ref, yzin_ref, *out_refs):
    sums_ref = out_refs[LEVELS]
    corner = yzin_ref[...]
    zface = jnp.concatenate([zin_ref[pl.ds(0, 8), :] + corner, zin_ref[pl.ds(8, COUNT[0] - 8), :]], axis=0)
    sums = jnp.zeros((1, LANES), jnp.float32)
    for level in range(LEVELS):
        count = COUNT[level]
        rows = max(count, 8)
        face_at = 32 if level else 0
        source = first_ref if level == 0 else rest_ref
        shape = (rows, LANES)
        inside = tile_mask(level, shape) & (iota(shape, 0) < count)
        zlane = iota(shape, 1) == LANE_AT[level]
        squares = jnp.zeros((8, LANES), jnp.float32)
        for plane in range(count):
            at = REST_AT[level] + plane * ROWS[level]
            values = source[pl.ds(at, rows), :]
            if plane == 0:
                values = values + xin_ref[pl.ds(face_at, rows), :]
            yrow = jnp.where(iota((8, LANES), 0) == 0, yin_ref[pl.ds(face_at + plane, 1), :], 0.0)
            if rows > 8:
                yrow = jnp.concatenate([yrow, jnp.zeros((rows - 8, LANES), jnp.float32)], axis=0)
            shift = (LANE_AT[level] - face_lane(level, plane)) % LANES
            zcol = zface[:rows]
            if shift:
                zcol = pltpu.roll(zcol, shift, 1)
            values = values + yrow + jnp.where(zlane, zcol, 0.0)
            if level:
                values = jnp.where(inside, values, 0.0)
            out_refs[level][plane] = values
            squared = values * values
            for tile in range(rows // 8):
                squares = squares + squared[tile * 8 : tile * 8 + 8]
        total = jnp.sum(jnp.sum(squares, axis=0, keepdims=True), axis=1, keepdims=True)
        sums = jnp.where(iota((1, LANES), 1) == level, total, sums)
    sums_ref[...] = jnp.broadcast_to(sums, sums_ref.shape)


def finish_levels(first, rest, xin, yin, zin, yzin, devices):
    f32 = jnp.float32
    vmem = pl.BlockSpec(memory_space=pltpu.VMEM)
    shapes = [(COUNT[level], max(COUNT[level], 8), LANES) for level in range(LEVELS)]
    shapes.append((devices, LANES))
    return pl.pallas_call(
        finish_kernel,
        out_shape=tuple(pltpu.VMEM(shape, f32) for shape in shapes),
        in_specs=[vmem] * 6,
        out_specs=(vmem,) * 6,
        name="finish",
    )(*resident(first, rest, xin, yin, zin, yzin))


def scale_kernel(sums_ref, *refs):
    level_refs = refs[:LEVELS]
    out_refs = refs[LEVELS : 2 * LEVELS]
    scales_ref = refs[2 * LEVELS]
    devices = sums_ref.shape[0]
    totals = jnp.sum(sums_ref[...], axis=0, keepdims=True)
    lane = iota((1, LANES), 1)
    square = jnp.ones((1, 1), jnp.float32)
    scales = jnp.zeros((1, LANES), jnp.float32)
    for level in range(LEVELS):
        cells = COUNT[level] * COUNT[level] * LANE_COUNT[level] * devices
        mean = jnp.sum(jnp.where(lane == level, totals, 0.0), axis=1, keepdims=True) * (1.0 / cells)
        before = square
        square = mean + EPSILON * before
        scale = jnp.sqrt(square / before)
        scales = jnp.where(lane == level, scale, scales)
        factor = jnp.broadcast_to(1.0 / jnp.sqrt(square), (8, LANES))
        count = COUNT[level]
        for plane in range(count):
            for tile in range(max(count // 8, 1)):
                values = level_refs[level][plane, pl.ds(tile * 8, 8), :] * factor
                if LANE_AT[level]:
                    values = pltpu.roll(values, LANES - LANE_AT[level], 1)
                size = min(count, 8)
                out_refs[level][plane, pl.ds(tile * 8, size), :] = values[:size, : LANE_COUNT[level]]
    scales_ref[...] = scales[0, :LEVELS]


def scale_levels(sums, levels):
    f32 = jnp.float32
    vmem = pl.BlockSpec(memory_space=pltpu.VMEM)
    shapes = [(COUNT[level], COUNT[level], LANE_COUNT[level]) for level in range(LEVELS)]
    shapes.append((LEVELS,))
    return pl.pallas_call(
        scale_kernel,
        out_shape=tuple(jax.ShapeDtypeStruct(shape, f32) for shape in shapes),
        in_specs=[vmem] * 6,
        out_specs=(vmem,) * 6,
        name="scale",
    )(*resident(sums, *levels))


def to_next(face, *axes):
    sizes = [lax.axis_size(axis) for axis in axes]
    route = []
    for source in range(math.prod(sizes)):
        target, rest, scale = 0, source, 1
        for size in reversed(sizes):
            target += (rest % size + 1) % size * scale
            rest //= size
            scale *= size
        route.append((source, target))
    return lax.ppermute(face, sum(axes, ()), route)


def per_device(residual_in):
    devices = lax.axis_size(GX_GY_GZ)
    high, highs, xface = high_half(residual_in)
    xin = to_next(xface, GX)
    first, rest, yface, zface = low_half(residual_in, high, highs)
    yface, zface, edge = add_edges(xin, yface, zface)
    edgein = to_next(edge, GY, GZ)
    zin = to_next(zface, GZ)
    yin = to_next(yface, GY)
    *levels, sums = finish_levels(first, rest, xin, yin, zin, edgein, devices)
    sums = lax.all_to_all(sums, GX_GY_GZ, 0, 0, tiled=True)
    return tuple(scale_levels(sums, levels))


def solution(mesh):
    torus = Mesh(
        mesh.devices.reshape(mesh.shape["gx"], mesh.shape["gy"] // 2, 2, mesh.shape["gz"]), GX_GY_GZ
    )
    placed = P("gx", GY, "gz")
    return jax.shard_map(
        per_device,
        mesh=torus,
        in_specs=(placed,),
        out_specs=(placed,) * LEVELS + (P(),),
        check_vma=False,
    )
```
